32 devices in a mesh: expert: 8 (over z, x), replica: 4 (over y, core).
Axes of the slice: x: 2, y: 2, z: 4, core: 2. Of those that a mesh axis runs over, the one named last changes fastest.
Arguments:
- tokens: bfloat16 [4096, 2048], P(('expert', 'replica')), may hold values from -6 to 6
- cotangent: bfloat16 [4096, 2048], P(('expert', 'replica')), may hold values from -6 to 6
- route_weights: float32 [4096, 8], P(('expert', 'replica')), may hold values from 0.02 to 0.4
- expert_ids: int32 [4096, 8], P(('expert', 'replica')), may hold values from 0 to 15, as said below
- slot_ids: int32 [4096, 8], P(('expert', 'replica')), may hold values from 0 to 63, as said below
- kept_mask: int32 [4096, 8], P(('expert', 'replica')), may hold values from 0 to 1, as said below
- gate_weight: bfloat16 [16, 2048, 384], P('expert'), may hold values from -0.125 to 0.125
- up_weight: bfloat16 [16, 2048, 384], P('expert'), may hold values from -0.125 to 0.125
- down_weight: bfloat16 [16, 384, 2048], P('expert'), may hold values from -0.3125 to 0.3125
- projector_basis: float32 [2048, 256], P('expert'), may hold values from -6 to 6
Outputs:
- token_grads: bfloat16 [4096, 2048], P(('expert', 'replica'))
- projected_grads: float32 [16, 3, 384, 256], P('expert')
- new_basis: float32 [2048, 256], P('expert')
The draws below stay inside these ranges and needn't reach their ends.
Inputs may be any that keep to these rules, and one draw needn't show every extreme that they name: `expert_ids`: each row names 8 different experts. `slot_ids`: within one device's rows, the kept routes to one expert take slots 0, 1, 2, ... in the order of rows and then of the position in the row; a dropped route has slot 0; in every draw some expert receives 64 kept routes from every device's rows. `kept_mask`: a route is dropped exactly when 64 earlier routes of the same device's rows go to the same expert.
All inputs are finite; a program needn't handle non-finite values.
Results may differ from the reference program's by a relative error of at most 0.019.
Values may be sent and summed in bfloat16 or wider, within the bound.
A program may use at most 128 MiB of HBM per device.

```python
import math
import jax
import jax.numpy as jnp
from jax import lax

D = 2048
TOP = 8
FF = 384
RANK = 256
TOK_DEV = 128
SPECIALIST_TOTAL = 16
CAP = 64
TOKENS = 4096
N_EXPERT = 8
N_REPLICA = 4


def routing_tables(key):
    key = jax.random.fold_in(key, 4242)
    noise_key, level_key, favored_key, coin_key = jax.random.split(key, 4)
    blocks = TOKENS // TOK_DEV
    stochastic_perturbation = jax.random.randint(noise_key, (TOKENS, SPECIALIST_TOTAL), 0, 4096)
    perturbation_magnitude = jax.random.randint(level_key, (SPECIALIST_TOTAL,), 0, 4) * 1024
    favorite_specialist = jax.random.randint(favored_key, (), 0, SPECIALIST_TOTAL)
    coin = jax.random.randint(coin_key, (TOKENS,), 0, 2)
    position = jnp.arange(TOKENS) % TOK_DEV
    chosen_specialists = jnp.logical_or(coin > 0, position < CAP)
    entry_positions = jnp.arange(SPECIALIST_TOTAL)[None, :]
    logit_increment = jnp.where(jnp.logical_and(chosen_specialists[:, None], entry_positions == favorite_specialist), 65536, 0)
    gating_logit = (stochastic_perturbation + perturbation_magnitude[None, :] + logit_increment) * SPECIALIST_TOTAL + entry_positions
    picked = lax.top_k(gating_logit, TOP)[1].astype(jnp.int32)
    onehot = (picked[:, :, None] == jnp.arange(SPECIALIST_TOTAL)[None, None, :]).astype(jnp.int32)
    onehot = onehot.reshape(blocks, TOK_DEV * TOP, SPECIALIST_TOTAL)
    running = jnp.cumsum(onehot, axis=1)
    ranking = (jnp.sum(onehot * running, axis=-1) - 1).reshape(TOKENS, TOP)
    kept = (ranking < CAP).astype(jnp.int32)
    slots = jnp.where(kept > 0, ranking, 0).astype(jnp.int32)
    return (picked, slots, kept)


def draw_expert_ids(key, part):
    return routing_tables(key)[0]


def draw_slot_ids(key, part):
    return routing_tables(key)[1]


def draw_kept_mask(key, part):
    return routing_tables(key)[2]


def raised(result, own_key, source, target, parts, factor):
    owner, partner = [(jnp.arange(result.shape[dim]) // (result.shape[dim] // parts)).reshape([-1 if axis == dim else 1 for axis in range(result.ndim)]) for dim in (source, target)]
    chosen = jax.random.permutation(own_key, parts)[partner]
    strong = (owner == chosen) | (owner == (partner + parts // 2) % parts)
    return jnp.where(strong, factor * result, result)


def levels(rng, dims, pieces, least, top_value):
    loudness = 1.0
    for dim, parts in pieces:
        steps = jax.random.uniform(jax.random.fold_in(jax.random.fold_in(rng, 6), dim), (parts,), jnp.float32, least / len(pieces), top_value / len(pieces))
        loudness = loudness * jnp.repeat(jnp.exp(steps), dims[dim] // parts).reshape((-1,) + (1,) * (len(dims) - 1 - dim))
    return loudness


def normal_values(own_key, dims, spread, bound, pieces=(), kind=jnp.bfloat16):
    result = spread * jax.random.normal(own_key, dims, jnp.float32)
    if pieces:
        result = result * levels(own_key, dims, pieces, -0.22, 0.18)
    return jnp.clip(result, -bound, bound).astype(kind)


def heavy_noise(rng, shape, deviation, bound, pieces, heavy, kind=jnp.bfloat16):
    result = deviation * jax.random.normal(rng, shape, jnp.float32)
    if pieces:
        result = result * levels(rng, shape, pieces, -0.22, 0.18)
    return jnp.clip(raised(result, jax.random.fold_in(rng, 3), *heavy), -bound, bound).astype(kind)


def setup_inputs(seed: int = 0) -> dict:
    keys = jax.random.split(jax.random.key(seed), 11)
    tokens = heavy_noise(keys[0], (TOKENS, D), 1.0, 6.0, ((0, 32),), (0, 1, 32, 2.75))
    cotangent = normal_values(keys[1], (TOKENS, D), 1.0, 6.0, ((0, 32),))
    route_weights = jnp.clip(0.02 + 0.38 * jax.random.uniform(keys[2], (TOKENS, TOP), jnp.float32) ** levels(keys[2], (TOKENS, TOP), ((0, 32),), -0.2, 0.2), 0.02, 0.4)
    expert_ids = draw_expert_ids(jax.random.fold_in(keys[10], 71), 0)
    slot_ids = draw_slot_ids(jax.random.fold_in(keys[10], 71), 0)
    kept_mask = draw_kept_mask(jax.random.fold_in(keys[10], 71), 0)
    gate_weight = normal_values(keys[6], (SPECIALIST_TOTAL, D, FF), D ** -0.5, 0.125, ((0, 8),))
    up_weight = normal_values(keys[7], (SPECIALIST_TOTAL, D, FF), D ** -0.5, 0.125, ((0, 8),))
    down_weight = normal_values(keys[8], (SPECIALIST_TOTAL, FF, D), FF ** -0.5, 0.3125, ((0, 8),))
    projector_basis = normal_values(keys[9], (D, RANK), 1.0, 6.0, ((0, 8),), jnp.float32)
    return {"tokens": tokens, "cotangent": cotangent, "route_weights": route_weights, "expert_ids": expert_ids, "slot_ids": slot_ids, "kept_mask": kept_mask, "gate_weight": gate_weight, "up_weight": up_weight, "down_weight": down_weight, "projector_basis": projector_basis}


def silu_parts(gate):
    sigma = jax.nn.sigmoid(gate)
    return (gate * sigma, sigma * (1.0 + gate * (1.0 - sigma)))

def rounded(value):
    return lax.optimization_barrier(value.astype(jnp.bfloat16)).astype(jnp.float32)

def reference(tokens, cotangent, route_weights, expert_ids, slot_ids, kept_mask, gate_weight, up_weight, down_weight, projector_basis):
    per_expert = N_EXPERT * CAP
    device_of = jnp.arange(TOKENS, dtype=jnp.int32) // TOK_DEV
    source_of = (device_of // N_REPLICA)[:, None]
    replica_of = (device_of % N_REPLICA)[:, None]
    empty_slot = SPECIALIST_TOTAL * N_REPLICA * per_expert
    target = jnp.where(kept_mask > 0, (expert_ids * N_REPLICA + replica_of) * per_expert + source_of * CAP + slot_ids, empty_slot).astype(jnp.int32)
    route_count = TOKENS * TOP
    table = jnp.full((empty_slot,), route_count, jnp.int32).at[target.reshape(-1)].set(jnp.arange(route_count, dtype=jnp.int32), mode='drop')
    table = table.reshape(SPECIALIST_TOTAL, N_REPLICA, per_expert)
    tokens_pad = jnp.concatenate([tokens, jnp.zeros((1, D), tokens.dtype)], 0)
    cotangent_pad = jnp.concatenate([cotangent, jnp.zeros((1, D), cotangent.dtype)], 0)
    weight_pad = jnp.concatenate([route_weights.reshape(-1), jnp.zeros((1,), route_weights.dtype)], 0)
    projector = rounded(projector_basis * (1.0 / math.sqrt(D)))

    def expert_step(power, inputs):
        routes, w_gate, w_up, w_down = inputs
        owner = routes // TOP
        x_rows = tokens_pad[owner].astype(jnp.float32)
        dy_rows = rounded(cotangent_pad[owner].astype(jnp.float32) * weight_pad[routes][..., None])
        gate_full = w_gate.astype(jnp.float32)
        up_full = w_up.astype(jnp.float32)
        gate = jnp.einsum('rpd,df->rpf', x_rows, gate_full)
        upper = jnp.einsum('rpd,df->rpf', x_rows, up_full)
        activated, slope = silu_parts(gate)
        hidden = rounded(activated * upper)
        hidden_grad = jnp.einsum('rpd,fd->rpf', dy_rows, w_down.astype(jnp.float32))
        up_grad = rounded(hidden_grad * activated)
        gate_grad = rounded(hidden_grad * upper * slope)
        row_grads = (jnp.einsum('rpf,df->rpd', gate_grad, gate_full) + jnp.einsum('rpf,df->rpd', up_grad, up_full)).astype(jnp.bfloat16)
        x_proj = rounded(jnp.einsum('rpd,dk->rpk', x_rows, projector))
        dy_proj = rounded(jnp.einsum('rpd,dk->rpk', dy_rows, projector))
        grads = jnp.stack([jnp.einsum('rpf,rpk->fk', gate_grad, x_proj), jnp.einsum('rpf,rpk->fk', up_grad, x_proj), jnp.einsum('rpf,rpk->fk', hidden, dy_proj)], 0)
        grads_low = rounded(grads)
        mixed = rounded(jnp.einsum('rpf,fk->rpk', gate_grad, grads_low[0]) + jnp.einsum('rpf,fk->rpk', up_grad, grads_low[1]))
        down_mix = rounded(jnp.einsum('rpf,fk->rpk', hidden, grads_low[2]))
        power = power + jnp.einsum('rpd,rpk->dk', x_rows, mixed) + jnp.einsum('rpd,rpk->dk', dy_rows, down_mix)
        return (power, (row_grads, grads))
    power, (row_grads, projected_grads) = lax.scan(expert_step, jnp.zeros((D, RANK), jnp.float32), (table, gate_weight, up_weight, down_weight))
    back = jnp.concatenate([row_grads.reshape(empty_slot, D), jnp.zeros((1, D), jnp.bfloat16)], 0)

    def combine(block_targets):
        return lax.optimization_barrier(jnp.sum(back[block_targets].astype(jnp.float32), axis=1)).astype(jnp.bfloat16)
    token_grads = lax.map(combine, target.reshape(TOKENS // TOK_DEV, TOK_DEV, TOP)).reshape(TOKENS, D)
    gram = jnp.dot(power.T.astype(jnp.float32), power.astype(jnp.float32), precision=lax.Precision.HIGHEST, preferred_element_type=jnp.float32)
    lower = jnp.linalg.cholesky(gram)
    new_basis = math.sqrt(D) * jax.scipy.linalg.solve_triangular(lower, power.T, lower=True).T
    return (token_grads, projected_grads, new_basis)
```

```python
import functools
import math

import jax
import jax.numpy as jnp
from jax import lax
from jax.experimental import pallas as pl
from jax.experimental.pallas import tpu as pltpu
from jax.sharding import PartitionSpec as P

F32 = jnp.float32
BF16 = jnp.bfloat16
HIGH = lax.Precision.HIGHEST


def solve_kernel(block, scale, gram_ref, panel_ref, out_ref, a_ref, y_ref):
    n = gram_ref.shape[0]
    a_ref[...] = gram_ref[...]
    y_ref[...] = panel_ref[...].T
    rows = lax.broadcasted_iota(jnp.int32, (block, 1), 0)
    eye = (
        lax.broadcasted_iota(jnp.int32, (block, block), 0)
        == lax.broadcasted_iota(jnp.int32, (block, block), 1)
    ).astype(F32)
    for step in range(n // block):
        own = pl.ds(step * block, block)
        work = jnp.concatenate([a_ref[own, step * block : (step + 1) * block], eye], 1)
        pivots = jnp.ones((block, 1), F32)
        for k in range(block):
            pivot = work[k : k + 1, k : k + 1]
            column = jnp.where(rows > k, work[:, k : k + 1], 0.0)
            pivots = jnp.where(rows == k, pivot, pivots)
            work = work - column * (work[k : k + 1, :] * (1.0 / pivot))
        inverse = work[:, block:] * (1.0 / jnp.sqrt(pivots))
        solved = jnp.dot(inverse, y_ref[own, :], precision=HIGH, preferred_element_type=F32)
        y_ref[own, :] = solved
        first = (step + 1) * block
        if first < n:
            upper = jnp.dot(
                inverse, a_ref[own, :], precision=HIGH, preferred_element_type=F32
            )
            lower = upper.T[first:, :]
            a_ref[first:, :] = a_ref[first:, :] - jnp.dot(
                lower, upper, precision=HIGH, preferred_element_type=F32
            )
            y_ref[first:, :] = y_ref[first:, :] - jnp.dot(
                lower, solved, precision=HIGH, preferred_element_type=F32
            )
    out_ref[...] = scale * y_ref[...].T


def solve_panel(gram, panel, scale):
    n = gram.shape[0]
    block = 64 if n % 64 == 0 else n
    vmem = pl.BlockSpec(memory_space=pltpu.VMEM)
    return pl.pallas_call(
        functools.partial(solve_kernel, block, scale),
        out_shape=jax.ShapeDtypeStruct(panel.shape, F32),
        in_specs=[vmem, vmem],
        out_specs=vmem,
        scratch_shapes=[pltpu.VMEM((n, n), F32), pltpu.VMEM((n, panel.shape[0]), F32)],
    )(gram, panel)


def gathered_body(
    tokens,
    cotangent,
    route_weights,
    expert_ids,
    slot_ids,
    kept_mask,
    gate_weight,
    up_weight,
    down_weight,
    projector_basis,
):
    tok_count, width = tokens.shape
    local_count = gate_weight.shape[0]
    groups = lax.axis_size("expert")
    replicas = lax.axis_size("replica")
    expert_total = local_count * groups
    slot_cap = tok_count * expert_ids.shape[1] // expert_total
    inner = 2
    outer = groups // inner
    me = lax.axis_index("expert")
    replica = lax.axis_index("replica")

    def shift(value, step):
        perm = [
            (e, ((e // inner + step) % outer) * inner + e % inner) for e in range(groups)
        ]
        return lax.ppermute(value, "expert", perm)

    def flip(value):
        return lax.ppermute(value, "expert", [(e, e ^ 1) for e in range(groups)])

    def gather(value):
        line = [value] + [shift(value, d) for d in range(1, outer)]
        return line + [flip(v) for v in line]

    line_ids = [((me // inner - d) % outer) * inner + me % inner for d in range(outer)]
    sources = line_ids + [i ^ 1 for i in line_ids]

    match = (expert_ids[None] == jnp.arange(expert_total)[:, None, None]) & (kept_mask[None] > 0)
    slot_map = jnp.max(jnp.where(match, slot_ids[None], -1), -1).astype(F32)
    weight_map = jnp.sum(jnp.where(match, route_weights[None], 0.0), -1)
    routes = jnp.stack(gather(jnp.concatenate([slot_map, weight_map], 0)))
    mine = me * local_count
    slots = lax.dynamic_slice_in_dim(routes, mine, local_count, 1).astype(jnp.int32)
    weights = lax.dynamic_slice_in_dim(routes, expert_total + mine, local_count, 1)
    taken = slots[:, :, None, :] == jnp.arange(slot_cap)[None, None, :, None]
    select = taken.astype(BF16)
    slot_weight = jnp.sum(jnp.where(taken, weights[:, :, None, :], 0.0), -1)

    x_blocks = jnp.stack(gather(tokens))
    basis_parts = gather((projector_basis * (1.0 / math.sqrt(width))).astype(BF16))
    dy_blocks = jnp.stack(gather(cotangent))
    panel = projector_basis.shape[0]
    projector = jnp.zeros((width, projector_basis.shape[1]), BF16)
    for source, part in zip(sources, basis_parts):
        projector = lax.dynamic_update_slice_in_dim(projector, part, source * panel, 0)

    def dot(spec, a, b):
        return jnp.einsum(spec, a, b, preferred_element_type=F32)

    x_rows = dot("sjct,std->jscd", select, x_blocks).astype(BF16)
    x_rows = x_rows.reshape(local_count, -1, width)
    gate = dot("jpd,jdf->jpf", x_rows, gate_weight)
    upper = dot("jpd,jdf->jpf", x_rows, up_weight)
    sigma = jax.nn.sigmoid(gate)
    activated = gate * sigma
    slope = sigma * (1.0 + gate * (1.0 - sigma))
    hidden = (activated * upper).astype(BF16)
    x_proj = dot("jpd,dr->jpr", x_rows, projector).astype(BF16)

    dy_rows = dot("sjct,std->jscd", select, dy_blocks)
    dy_rows = (dy_rows * slot_weight.transpose(1, 0, 2)[..., None]).astype(BF16)
    dy_rows = dy_rows.reshape(local_count, -1, width)
    hidden_grad = dot("jpd,jfd->jpf", dy_rows, down_weight)
    up_grad = (hidden_grad * activated).astype(BF16)
    gate_grad = (hidden_grad * upper * slope).astype(BF16)
    dy_proj = dot("jpd,dr->jpr", dy_rows, projector).astype(BF16)

    partial = jnp.stack(
        [
            dot("jpf,jpr->jfr", gate_grad, x_proj),
            dot("jpf,jpr->jfr", up_grad, x_proj),
            dot("jpf,jpr->jfr", hidden, dy_proj),
        ],
        1,
    )

    def swap(value, bit):
        return lax.ppermute(value, "replica", [(r, r ^ bit) for r in range(replicas)])

    halves = partial.reshape(2, -1, partial.shape[-1])
    core = replica % 2
    half = lax.dynamic_index_in_dim(halves, core, 0, False) + swap(
        lax.dynamic_index_in_dim(halves, 1 - core, 0, False), 1
    )
    bit = 2
    while bit < replicas:
        low = half.astype(BF16)
        half = low.astype(F32) + swap(low, bit).astype(F32)
        bit *= 2
    other = swap(half, 1)
    projected_grads = jnp.where(
        core == 0, jnp.stack([half, other]), jnp.stack([other, half])
    ).reshape(partial.shape)

    row_grads = dot("jpf,jdf->jpd", gate_grad, gate_weight) + dot(
        "jpf,jdf->jpd", up_grad, up_weight
    )
    row_grads = row_grads.astype(BF16).reshape(local_count, groups, slot_cap, width)
    back = dot("sjct,jscd->std", select, row_grads).astype(BF16)
    total = None
    for d in range(outer):
        pair = back[d].astype(F32) + flip(back[outer + d]).astype(F32)
        if d:
            pair = shift(pair.astype(BF16), -d).astype(F32)
        total = pair if total is None else total + pair
    token_grads = total.astype(BF16)

    grads_low = projected_grads.astype(BF16)
    mixed = dot("jpf,jfr->jpr", gate_grad, grads_low[:, 0])
    mixed = (mixed + dot("jpf,jfr->jpr", up_grad, grads_low[:, 1])).astype(BF16)
    down_mix = dot("jpf,jfr->jpr", hidden, grads_low[:, 2]).astype(BF16)
    power = dot("jpd,jpr->dr", x_rows, mixed) + dot("jpd,jpr->dr", dy_rows, down_mix)

    rank = power.shape[-1]
    piece = power.reshape(groups, replicas, panel // replicas, rank)
    bit = 1
    while bit < replicas:
        piece = piece.reshape(groups, -1, 2, panel // replicas, rank)
        keep = (replica // bit) % 2
        kept = lax.dynamic_index_in_dim(piece, keep, 2, False)
        sent = lax.dynamic_index_in_dim(piece, 1 - keep, 2, False)
        piece = kept + swap(sent, bit)
        bit *= 2
    piece = piece.reshape(outer, inner, panel // replicas, rank)
    side = me % inner
    piece = lax.dynamic_index_in_dim(piece, side, 1, False) + flip(
        lax.dynamic_index_in_dim(piece, 1 - side, 1, False)
    )
    mine_z = me // inner
    own = lax.dynamic_index_in_dim(piece, mine_z, 0, False)
    for d in range(1, outer):
        own = own + shift(
            lax.dynamic_index_in_dim(piece, (mine_z + d) % outer, 0, False), d
        )
    own = own[None]
    bit = replicas // 2
    while bit >= 1:
        theirs = swap(own, bit)
        first = (replica // bit) % 2 == 0
        own = jnp.where(first, jnp.stack([own, theirs], 1), jnp.stack([theirs, own], 1))
        own = own.reshape(-1, panel // replicas, rank)
        bit //= 2
    own_panel = own.reshape(panel, rank)
    gram = jnp.dot(own_panel.T, own_panel, precision=HIGH, preferred_element_type=F32)
    bit = 1
    gram = gram + flip(gram)
    step = 1
    while step < outer:
        perm = [(e, e ^ (step * inner)) for e in range(groups)]
        gram = gram + lax.ppermute(gram, "expert", perm)
        step *= 2
    new_basis = solve_panel(gram, own_panel, math.sqrt(width))
    return (token_grads, projected_grads, new_basis)


def routed_body(
    tokens,
    cotangent,
    route_weights,
    expert_ids,
    slot_ids,
    kept_mask,
    gate_weight,
    up_weight,
    down_weight,
    projector_basis,
):
    tok_count, model_width = tokens.shape
    route_top = expert_ids.shape[1]
    local_count = gate_weight.shape[0]
    group_count = lax.axis_size("expert")
    expert_total = local_count * group_count
    slot_cap = tok_count * route_top // expert_total
    slot_total = expert_total * slot_cap
    route_count = tok_count * route_top
    target = jnp.where(kept_mask > 0, expert_ids * slot_cap + slot_ids, slot_total).reshape(-1)
    table = (
        jnp.full((slot_total,), route_count, jnp.int32)
        .at[target]
        .set(jnp.arange(route_count, dtype=jnp.int32), mode="drop")
    )
    owner = table // route_top
    tokens_pad = jnp.concatenate([tokens, jnp.zeros((1, model_width), tokens.dtype)], 0)
    cotangent_pad = jnp.concatenate([cotangent, jnp.zeros((1, model_width), cotangent.dtype)], 0)
    weight_pad = jnp.concatenate([route_weights.reshape(-1), jnp.zeros((1,), jnp.float32)], 0)
    x_send = tokens_pad[owner].reshape(group_count, local_count * slot_cap, model_width)
    dy_send = (cotangent_pad[owner].astype(jnp.float32) * weight_pad[table][:, None]).astype(
        jnp.bfloat16
    )
    dy_send = dy_send.reshape(group_count, local_count * slot_cap, model_width)
    full_basis = lax.all_gather(
        projector_basis.astype(jnp.bfloat16), "expert", axis=0, tiled=True
    ).astype(projector_basis.dtype)
    projector = (full_basis * (1.0 / math.sqrt(model_width))).astype(jnp.bfloat16)
    block_shape = (group_count, local_count, slot_cap, model_width)
    x_recv, dy_recv = (
        lax.all_to_all(x_send, "expert", split_axis=0, concat_axis=0, tiled=True),
        lax.all_to_all(dy_send, "expert", split_axis=0, concat_axis=0, tiled=True),
    )
    x_rows = x_recv.reshape(block_shape)
    gate = jnp.einsum("sjcd,jdf->sjcf", x_rows, gate_weight, preferred_element_type=jnp.float32)
    upper = jnp.einsum("sjcd,jdf->sjcf", x_rows, up_weight, preferred_element_type=jnp.float32)
    sigma = jax.nn.sigmoid(gate)
    activated = gate * sigma
    slope = sigma * (1.0 + gate * (1.0 - sigma))
    hidden = (activated * upper).astype(jnp.bfloat16)
    x_proj = jnp.einsum(
        "sjcd,dr->sjcr", x_rows, projector, preferred_element_type=jnp.float32
    ).astype(jnp.bfloat16)
    x_rows, upper, activated, slope, hidden, x_proj = (
        x_rows,
        upper,
        activated,
        slope,
        hidden,
        x_proj,
    )
    dy_rows = dy_recv.reshape(block_shape)
    hidden_grad = jnp.einsum(
        "sjcd,jfd->sjcf", dy_rows, down_weight, preferred_element_type=jnp.float32
    )
    up_grad = (hidden_grad * activated).astype(jnp.bfloat16)
    gate_grad = (hidden_grad * upper * slope).astype(jnp.bfloat16)
    row_grads = jnp.einsum(
        "sjcf,jdf->sjcd", gate_grad, gate_weight, preferred_element_type=jnp.float32
    )
    row_grads = row_grads + jnp.einsum(
        "sjcf,jdf->sjcd", up_grad, up_weight, preferred_element_type=jnp.float32
    )
    row_grads = row_grads.astype(jnp.bfloat16).reshape(
        group_count, local_count * slot_cap, model_width
    )
    returned = lax.all_to_all(row_grads, "expert", split_axis=0, concat_axis=0, tiled=True).reshape(
        slot_total, model_width
    )
    returned = jnp.concatenate([returned, jnp.zeros((1, model_width), jnp.bfloat16)], 0)
    token_grads = jnp.sum(
        returned[target].reshape(tok_count, route_top, model_width).astype(jnp.float32), axis=1
    ).astype(jnp.bfloat16)
    dy_proj = jnp.einsum(
        "sjcd,dr->sjcr", dy_rows, projector, preferred_element_type=jnp.float32
    ).astype(jnp.bfloat16)
    partial_grads = jnp.stack(
        [
            jnp.einsum("sjcf,sjcr->jfr", gate_grad, x_proj, preferred_element_type=jnp.float32),
            jnp.einsum("sjcf,sjcr->jfr", up_grad, x_proj, preferred_element_type=jnp.float32),
            jnp.einsum("sjcf,sjcr->jfr", hidden, dy_proj, preferred_element_type=jnp.float32),
        ],
        1,
    )
    projected_grads = lax.psum(partial_grads, "replica")
    grads_low = projected_grads.astype(jnp.bfloat16)
    mixed = jnp.einsum(
        "sjcf,jfr->sjcr", gate_grad, grads_low[:, 0], preferred_element_type=jnp.float32
    )
    mixed = (
        mixed
        + jnp.einsum("sjcf,jfr->sjcr", up_grad, grads_low[:, 1], preferred_element_type=jnp.float32)
    ).astype(jnp.bfloat16)
    down_mix = jnp.einsum(
        "sjcf,jfr->sjcr", hidden, grads_low[:, 2], preferred_element_type=jnp.float32
    ).astype(jnp.bfloat16)
    power = jnp.einsum("sjcd,sjcr->dr", x_rows, mixed, preferred_element_type=jnp.float32)
    power = power + jnp.einsum(
        "sjcd,sjcr->dr", dy_rows, down_mix, preferred_element_type=jnp.float32
    )
    panel_rows = model_width // group_count
    power_sum = lax.psum(power, ("expert", "replica"))
    gram_total = jnp.dot(
        power_sum.T, power_sum, precision=lax.Precision.HIGHEST, preferred_element_type=jnp.float32
    )
    own_panel = lax.dynamic_slice_in_dim(
        power_sum, lax.axis_index("expert") * panel_rows, panel_rows, 0
    )
    lower = jnp.linalg.cholesky(gram_total)
    new_basis = (
        math.sqrt(model_width) * jax.scipy.linalg.solve_triangular(lower, own_panel.T, lower=True).T
    )
    return (token_grads, projected_grads, new_basis)


def power_of_two(count):
    return count > 1 and count & (count - 1) == 0


def body(*args):
    tok_count, local_count = args[0].shape[0], args[6].shape[0]
    groups, replicas = lax.axis_size("expert"), lax.axis_size("replica")
    slot_cap = tok_count * args[3].shape[1] // (local_count * groups)
    if (
        local_count * slot_cap >= tok_count
        and power_of_two(groups)
        and power_of_two(replicas)
    ):
        return gathered_body(*args)
    return routed_body(*args)


def solution(mesh):
    return jax.shard_map(
        body,
        mesh=mesh,
        in_specs=(
            P(("expert", "replica"), None),
            P(("expert", "replica"), None),
            P(("expert", "replica"), None),
            P(("expert", "replica"), None),
            P(("expert", "replica"), None),
            P(("expert", "replica"), None),
            P("expert", None, None),
            P("expert", None, None),
            P("expert", None, None),
            P("expert", None),
        ),
        out_specs=(
            P(("expert", "replica"), None),
            P("expert", None, None, None),
            P("expert", None),
        ),
        check_vma=False,
    )
```

```python
import functools
import math

import jax
import jax.numpy as jnp
from jax import lax
from jax.experimental import pallas as pl
from jax.experimental.pallas import tpu as pltpu
from jax.sharding import PartitionSpec as P

F32 = jnp.float32
BF16 = jnp.bfloat16
HIGH = lax.Precision.HIGHEST


MESH = pl.DeviceIdType.MESH


def solve_rows(block, scale, out_ref, a_ref, y_ref):
    n = a_ref.shape[0]
    rows = lax.broadcasted_iota(jnp.int32, (block, 1), 0)
    eye = (
        lax.broadcasted_iota(jnp.int32, (block, block), 0)
        == lax.broadcasted_iota(jnp.int32, (block, block), 1)
    ).astype(F32)
    for step in range(n // block):
        own = pl.ds(step * block, block)
        work = jnp.concatenate([a_ref[own, step * block : (step + 1) * block], eye], 1)
        pivots = jnp.ones((block, 1), F32)
        for k in range(block):
            pivot = work[k : k + 1, k : k + 1]
            column = jnp.where(rows > k, work[:, k : k + 1], 0.0)
            pivots = jnp.where(rows == k, pivot, pivots)
            work = work - column * (work[k : k + 1, :] * (1.0 / pivot))
        inverse = work[:, block:] * (1.0 / jnp.sqrt(pivots))
        solved = jnp.dot(inverse, y_ref[own, :], precision=HIGH, preferred_element_type=F32)
        y_ref[own, :] = solved
        first = (step + 1) * block
        if first < n:
            upper = jnp.dot(
                inverse, a_ref[own, :], precision=HIGH, preferred_element_type=F32
            )
            lower = upper.T[first:, :]
            a_ref[first:, :] = a_ref[first:, :] - jnp.dot(
                lower, upper, precision=HIGH, preferred_element_type=F32
            )
            y_ref[first:, :] = y_ref[first:, :] - jnp.dot(
                lower, solved, precision=HIGH, preferred_element_type=F32
            )
    out_ref[...] = scale * y_ref[...].T


def greet(expert_peers, replica_peers):
    barrier = pltpu.get_barrier_semaphore()
    for peer in expert_peers:
        pl.semaphore_signal(barrier, inc=1, device_id={"expert": peer}, device_id_type=MESH)
    for peer in replica_peers:
        pl.semaphore_signal(barrier, inc=1, device_id={"replica": peer}, device_id_type=MESH)
    pl.semaphore_wait(barrier, len(expert_peers) + len(replica_peers))


def line_peer(me, outer, inner, step):
    return lax.rem(me // inner + step + outer, outer) * inner + lax.rem(me, inner)


def gather_kernel(
    groups,
    chunks,
    tok_ref,
    cot_ref,
    route_ref,
    basis_ref,
    tok_out,
    cot_out,
    route_out,
    basis_out,
    send_sem,
    recv_sem,
    own_sem,
):
    inner = 2
    outer = groups // inner
    me = lax.axis_index("expert")
    ahead = [line_peer(me, outer, inner, d) for d in range(outer)]
    behind = [line_peer(me, outer, inner, -d) for d in range(outer)]
    side = me + 1 - 2 * lax.rem(me, inner)
    greet(ahead[1:] + [side], [])

    own = [
        pltpu.make_async_copy(src, dst.at[me], own_sem.at[i])
        for i, (src, dst) in enumerate(
            (
                (tok_ref, tok_out),
                (cot_ref, cot_out),
                (route_ref, route_out),
                (basis_ref, basis_out),
            )
        )
    ]
    rows = tok_ref.shape[0] // chunks
    parts = [(route_ref, route_out, None)]
    parts += [(tok_ref, tok_out, pl.ds(c * rows, rows)) for c in range(chunks)]
    parts += [(basis_ref, basis_out, None)]
    parts += [(cot_ref, cot_out, pl.ds(c * rows, rows)) for c in range(chunks)]

    def copy(i, lane, source, target):
        src, dst, span = parts[i]
        if source is None:
            here = src if span is None else src.at[span]
            row = me
        else:
            here = dst.at[source] if span is None else dst.at[source, span]
            row = source
        there = dst.at[row] if span is None else dst.at[row, span]
        return pltpu.make_async_remote_copy(
            src_ref=here,
            dst_ref=there,
            send_sem=send_sem.at[i, lane],
            recv_sem=recv_sem.at[i, lane],
            device_id={"expert": target},
            device_id_type=MESH,
        )

    started = []

    def relay(i):
        for d in range(1, outer):
            line[i][d - 1].wait_recv()
            onward = copy(i, outer - 1 + d, behind[d], side)
            onward.start()
            started.append(onward)

    line = []
    flips = []
    for i in range(len(parts)):
        flips.append(copy(i, outer - 1, None, side))
        flips[-1].start()
        line.append([copy(i, d - 1, None, ahead[d]) for d in range(1, outer)])
        for c in line[-1]:
            c.start()
        if i >= 2:
            relay(i - 2)
        if i == 0:
            for c in own:
                c.start()
    for i in range(max(len(parts) - 2, 0), len(parts)):
        relay(i)
    for c in own:
        c.wait()
    for i in range(len(parts)):
        for c in line[i]:
            c.wait_send()
    for c in flips + started:
        c.wait()


def gather_all(tokens, cotangent, routes, basis):
    groups = lax.axis_size("expert")
    chunks = 4 if tokens.shape[0] % 64 == 0 else 1
    vmem = pl.BlockSpec(memory_space=pltpu.VMEM)
    arrays = (tokens, cotangent, routes, basis)
    count = 2 + 2 * chunks
    lanes = groups - 1
    return pl.pallas_call(
        functools.partial(gather_kernel, groups, chunks),
        out_shape=[jax.ShapeDtypeStruct((groups,) + a.shape, a.dtype) for a in arrays],
        in_specs=[vmem] * 4,
        out_specs=[pl.BlockSpec(memory_space=pl.ANY)] * 4,
        scratch_shapes=[
            pltpu.SemaphoreType.DMA((count, lanes)),
            pltpu.SemaphoreType.DMA((count, lanes)),
            pltpu.SemaphoreType.DMA((4,)),
        ],
        compiler_params=pltpu.CompilerParams(collective_id=0, has_side_effects=True),
    )(*arrays)


def finish_kernel(
    groups,
    scale,
    power_ref,
    out_ref,
    half_in,
    half_sum,
    low_out,
    low_in,
    own_sum,
    side_out,
    side_in,
    pair_sum,
    line_out,
    line_in,
    panel_ref,
    gram_part,
    gram_in,
    gram_ref,
    a_ref,
    y_ref,
    send_sem,
    recv_sem,
    gather_send,
    gather_recv,
):
    inner = 2
    outer = groups // inner
    me = lax.axis_index("expert")
    replica = lax.axis_index("replica")
    core = lax.rem(replica, 2)
    row = replica // 2
    twin = replica + 1 - 2 * core
    across = replica + 2 - 4 * row
    place = lax.rem(me, inner)
    depth = me // inner
    side = me + 1 - 2 * place
    peers = [lax.rem(me + d, groups) for d in range(groups)]
    greet(peers[1:], [twin, across])
    rows, rank = power_ref.shape[3:]

    def send(src, dst, sem, target):
        return pltpu.make_async_remote_copy(
            src_ref=src,
            dst_ref=dst,
            send_sem=send_sem.at[sem],
            recv_sem=recv_sem.at[sem],
            device_id=target,
            device_id_type=MESH,
        )

    step = send(power_ref.at[:, 1 - core], half_in, 0, {"replica": twin})
    step.start()
    step.wait()
    half_sum[...] = power_ref[:, core] + half_in[...]
    low_out[...] = half_sum[:, 1 - row].astype(BF16)
    step = send(low_out, low_in, 1, {"replica": across})
    step.start()
    step.wait()
    own_sum[...] = half_sum[:, row] + low_in[...].astype(F32)
    for z in range(outer):
        side_out[z] = own_sum[z * inner + 1 - place].astype(BF16)
    step = send(side_out, side_in, 2, {"expert": side})
    step.start()
    step.wait()
    for z in range(outer):
        pair_sum[z] = own_sum[z * inner + place] + side_in[z].astype(F32)
    line_out[...] = pair_sum[...].astype(BF16)
    steps = []
    for d in range(1, outer):
        target = lax.rem(depth + d, outer)
        steps.append(
            send(
                line_out.at[target],
                line_in.at[d - 1],
                2 + d,
                {"expert": target * inner + place},
            )
        )
    for step in steps:
        step.start()
    for step in steps:
        step.wait()
    total = pair_sum[depth]
    for d in range(1, outer):
        total = total + line_in[d - 1].astype(F32)
    panel_ref[core, row] = total
    step = send(
        panel_ref.at[core, row], panel_ref.at[core, row], 2 + outer, {"replica": across}
    )
    step.start()
    step.wait()
    step = send(panel_ref.at[core], panel_ref.at[core], 3 + outer, {"replica": twin})
    step.start()
    step.wait()
    panel = panel_ref[...].reshape(4 * rows, rank)
    wide = rank // 4
    y_ref[...] = panel.T
    quarter = core * 2 + row
    part = jnp.dot(
        y_ref[pl.ds(pl.multiple_of(quarter * wide, wide), wide), :],
        panel,
        precision=HIGH,
        preferred_element_type=F32,
    )
    thin = wide // groups
    gram_part[...] = part.reshape(groups, thin, rank)

    def spread(src, dst, stage, d):
        return pltpu.make_async_remote_copy(
            src_ref=src,
            dst_ref=dst,
            send_sem=gather_send.at[stage, d - 1],
            recv_sem=gather_recv.at[stage, d - 1],
            device_id={"expert": peers[d]},
            device_id_type=MESH,
        )

    steps = [
        spread(gram_part.at[peers[d]], gram_in.at[d - 1], 0, d) for d in range(1, groups)
    ]
    for step in steps:
        step.start()
    for step in steps:
        step.wait()
    whole = gram_part[me]
    for d in range(1, groups):
        whole = whole + gram_in[d - 1]
    gram_ref[core, row, me] = whole
    mine = gram_ref.at[core, row, me]
    steps = [spread(mine, mine, 1, d) for d in range(1, groups)]
    for step in steps:
        step.start()
    for step in steps:
        step.wait()
    mine = gram_ref.at[core, row]
    step = send(mine, mine, 4 + outer, {"replica": across})
    step.start()
    step.wait()
    mine = gram_ref.at[core]
    step = send(mine, mine, 5 + outer, {"replica": twin})
    step.start()
    step.wait()
    a_ref[...] = gram_ref[...].reshape(rank, rank)
    solve_rows(64, scale, out_ref, a_ref, y_ref)


def finish(power, groups, scale):
    width, rank = power.shape
    rows = width // groups // 4
    outer = groups // 2
    vmem = pl.BlockSpec(memory_space=pltpu.VMEM)
    wide = rank // 4
    return pl.pallas_call(
        functools.partial(finish_kernel, groups, scale),
        out_shape=jax.ShapeDtypeStruct((4 * rows, rank), F32),
        in_specs=[vmem],
        out_specs=vmem,
        scratch_shapes=[
            pltpu.VMEM((groups, 2, rows, rank), F32),
            pltpu.VMEM((groups, 2, rows, rank), F32),
            pltpu.VMEM((groups, rows, rank), BF16),
            pltpu.VMEM((groups, rows, rank), BF16),
            pltpu.VMEM((groups, rows, rank), F32),
            pltpu.VMEM((outer, rows, rank), BF16),
            pltpu.VMEM((outer, rows, rank), BF16),
            pltpu.VMEM((outer, rows, rank), F32),
            pltpu.VMEM((outer, rows, rank), BF16),
            pltpu.VMEM((outer - 1, rows, rank), BF16),
            pltpu.VMEM((2, 2, rows, rank), F32),
            pltpu.VMEM((groups, wide // groups, rank), F32),
            pltpu.VMEM((groups - 1, wide // groups, rank), F32),
            pltpu.VMEM((2, 2, groups, wide // groups, rank), F32),
            pltpu.VMEM((rank, rank), F32),
            pltpu.VMEM((rank, 4 * rows), F32),
            pltpu.SemaphoreType.DMA((6 + outer,)),
            pltpu.SemaphoreType.DMA((6 + outer,)),
            pltpu.SemaphoreType.DMA((2, groups - 1)),
            pltpu.SemaphoreType.DMA((2, groups - 1)),
        ],
        compiler_params=pltpu.CompilerParams(collective_id=1, has_side_effects=True),
        cost_estimate=pl.CostEstimate(
            flops=40_000_000_000, bytes_accessed=100_000_000, transcendentals=0
        ),
    )(power.reshape(groups, 2, 2, rows, rank))


def gathered_body(
    tokens,
    cotangent,
    route_weights,
    expert_ids,
    slot_ids,
    kept_mask,
    gate_weight,
    up_weight,
    down_weight,
    projector_basis,
):
    tok_count, width = tokens.shape
    local_count = gate_weight.shape[0]
    groups = lax.axis_size("expert")
    replicas = lax.axis_size("replica")
    expert_total = local_count * groups
    slot_cap = tok_count * expert_ids.shape[1] // expert_total
    inner = 2
    outer = groups // inner
    me = lax.axis_index("expert")
    replica = lax.axis_index("replica")

    def shift(value, step):
        perm = [
            (e, ((e // inner + step) % outer) * inner + e % inner) for e in range(groups)
        ]
        return lax.ppermute(value, "expert", perm)

    def flip(value):
        return lax.ppermute(value, "expert", [(e, e ^ 1) for e in range(groups)])

    match = (expert_ids[None] == jnp.arange(expert_total)[:, None, None]) & (kept_mask[None] > 0)
    slot_map = jnp.max(jnp.where(match, slot_ids[None], -1), -1).astype(F32)
    weight_map = jnp.sum(jnp.where(match, route_weights[None], 0.0), -1)
    x_blocks, dy_blocks, routes, projector = gather_all(
        tokens,
        cotangent,
        jnp.concatenate([slot_map, weight_map], 0),
        (projector_basis * (1.0 / math.sqrt(width))).astype(BF16),
    )
    projector = projector.reshape(width, -1)
    mine = me * local_count
    slots = lax.dynamic_slice_in_dim(routes, mine, local_count, 1).astype(jnp.int32)
    weights = lax.dynamic_slice_in_dim(routes, expert_total + mine, local_count, 1)
    taken = slots[:, :, None, :] == jnp.arange(slot_cap)[None, None, :, None]
    select = taken.astype(BF16)
    slot_weight = jnp.sum(jnp.where(taken, weights[:, :, None, :], 0.0), -1)

    def dot(spec, a, b):
        return jnp.einsum(spec, a, b, preferred_element_type=F32)

    x_rows = dot("sjct,std->jscd", select, x_blocks).astype(BF16)
    x_rows = x_rows.reshape(local_count, -1, width)
    gate = dot("jpd,jdf->jpf", x_rows, gate_weight)
    upper = dot("jpd,jdf->jpf", x_rows, up_weight)
    sigma = jax.nn.sigmoid(gate)
    activated = gate * sigma
    slope = sigma * (1.0 + gate * (1.0 - sigma))
    hidden = (activated * upper).astype(BF16)
    x_proj = dot("jpd,dr->jpr", x_rows, projector).astype(BF16)

    dy_rows = dot("sjct,std->jscd", select, dy_blocks)
    dy_rows = (dy_rows * slot_weight.transpose(1, 0, 2)[..., None]).astype(BF16)
    dy_rows = dy_rows.reshape(local_count, -1, width)
    hidden_grad = dot("jpd,jfd->jpf", dy_rows, down_weight)
    up_grad = (hidden_grad * activated).astype(BF16)
    gate_grad = (hidden_grad * upper * slope).astype(BF16)
    dy_proj = dot("jpd,dr->jpr", dy_rows, projector).astype(BF16)

    row_grads = dot("jpf,jdf->jpd", gate_grad, gate_weight) + dot(
        "jpf,jdf->jpd", up_grad, up_weight
    )
    row_grads = row_grads.astype(BF16).reshape(local_count, groups, slot_cap, width)
    back = dot("sjct,jscd->std", select, row_grads).astype(BF16)
    back = back.reshape(outer, inner, tok_count, width)
    place, depth = me % inner, me // inner
    stay, leave = [], []
    for d in range(outer):
        pair = lax.dynamic_index_in_dim(back, (depth + d) % outer, 0, False)
        stay.append(lax.dynamic_index_in_dim(pair, place, 0, False))
        leave.append(lax.dynamic_index_in_dim(pair, 1 - place, 0, False))
    leave, gate_grad, up_grad, hidden = lax.optimization_barrier(
        (leave, gate_grad, up_grad, hidden)
    )
    arrived = [flip(v) for v in leave]

    partial = jnp.stack(
        [
            dot("jpf,jpr->jfr", gate_grad, x_proj),
            dot("jpf,jpr->jfr", up_grad, x_proj),
            dot("jpf,jpr->jfr", hidden, dy_proj),
        ],
        1,
    )

    def swap(value, bit):
        return lax.ppermute(value, "replica", [(r, r ^ bit) for r in range(replicas)])

    halves = partial.reshape(2, -1, partial.shape[-1])
    core = replica % 2
    half = lax.dynamic_index_in_dim(halves, core, 0, False) + swap(
        lax.dynamic_index_in_dim(halves, 1 - core, 0, False), 1
    )
    bit = 2
    while bit < replicas:
        low = half.astype(BF16)
        half = low.astype(F32) + swap(low, bit).astype(F32)
        bit *= 2
    other = swap(half, 1)
    projected_grads = jnp.where(
        core == 0, jnp.stack([half, other]), jnp.stack([other, half])
    ).reshape(partial.shape)

    grads_low = projected_grads.astype(BF16)
    mixed = dot("jpf,jfr->jpr", gate_grad, grads_low[:, 0])
    mixed = (mixed + dot("jpf,jfr->jpr", up_grad, grads_low[:, 1])).astype(BF16)
    down_mix = dot("jpf,jfr->jpr", hidden, grads_low[:, 2]).astype(BF16)
    power = dot("jpd,jpr->dr", x_rows, mixed) + dot("jpd,jpr->dr", dy_rows, down_mix)

    pairs = [a.astype(F32) + b.astype(F32) for a, b in zip(stay, arrived)]
    sent = [p.astype(BF16) for p in pairs[1:]]
    sent, power = lax.optimization_barrier((sent, power))
    new_basis = finish(power, groups, math.sqrt(width))
    total = pairs[0]
    for d in range(1, outer):
        total = total + shift(sent[d - 1], d).astype(F32)
    token_grads = total.astype(BF16)
    return (token_grads, projected_grads, new_basis)


def routed_body(
    tokens,
    cotangent,
    route_weights,
    expert_ids,
    slot_ids,
    kept_mask,
    gate_weight,
    up_weight,
    down_weight,
    projector_basis,
):
    tok_count, model_width = tokens.shape
    route_top = expert_ids.shape[1]
    local_count = gate_weight.shape[0]
    group_count = lax.axis_size("expert")
    expert_total = local_count * group_count
    slot_cap = tok_count * route_top // expert_total
    slot_total = expert_total * slot_cap
    route_count = tok_count * route_top
    target = jnp.where(kept_mask > 0, expert_ids * slot_cap + slot_ids, slot_total).reshape(-1)
    table = (
        jnp.full((slot_total,), route_count, jnp.int32)
        .at[target]
        .set(jnp.arange(route_count, dtype=jnp.int32), mode="drop")
    )
    owner = table // route_top
    tokens_pad = jnp.concatenate([tokens, jnp.zeros((1, model_width), tokens.dtype)], 0)
    cotangent_pad = jnp.concatenate([cotangent, jnp.zeros((1, model_width), cotangent.dtype)], 0)
    weight_pad = jnp.concatenate([route_weights.reshape(-1), jnp.zeros((1,), jnp.float32)], 0)
    x_send = tokens_pad[owner].reshape(group_count, local_count * slot_cap, model_width)
    dy_send = (cotangent_pad[owner].astype(jnp.float32) * weight_pad[table][:, None]).astype(
        jnp.bfloat16
    )
    dy_send = dy_send.reshape(group_count, local_count * slot_cap, model_width)
    full_basis = lax.all_gather(
        projector_basis.astype(jnp.bfloat16), "expert", axis=0, tiled=True
    ).astype(projector_basis.dtype)
    projector = (full_basis * (1.0 / math.sqrt(model_width))).astype(jnp.bfloat16)
    block_shape = (group_count, local_count, slot_cap, model_width)
    x_recv, dy_recv = (
        lax.all_to_all(x_send, "expert", split_axis=0, concat_axis=0, tiled=True),
        lax.all_to_all(dy_send, "expert", split_axis=0, concat_axis=0, tiled=True),
    )
    x_rows = x_recv.reshape(block_shape)
    gate = jnp.einsum("sjcd,jdf->sjcf", x_rows, gate_weight, preferred_element_type=jnp.float32)
    upper = jnp.einsum("sjcd,jdf->sjcf", x_rows, up_weight, preferred_element_type=jnp.float32)
    sigma = jax.nn.sigmoid(gate)
    activated = gate * sigma
    slope = sigma * (1.0 + gate * (1.0 - sigma))
    hidden = (activated * upper).astype(jnp.bfloat16)
    x_proj = jnp.einsum(
        "sjcd,dr->sjcr", x_rows, projector, preferred_element_type=jnp.float32
    ).astype(jnp.bfloat16)
    x_rows, upper, activated, slope, hidden, x_proj = (
        x_rows,
        upper,
        activated,
        slope,
        hidden,
        x_proj,
    )
    dy_rows = dy_recv.reshape(block_shape)
    hidden_grad = jnp.einsum(
        "sjcd,jfd->sjcf", dy_rows, down_weight, preferred_element_type=jnp.float32
    )
    up_grad = (hidden_grad * activated).astype(jnp.bfloat16)
    gate_grad = (hidden_grad * upper * slope).astype(jnp.bfloat16)
    row_grads = jnp.einsum(
        "sjcf,jdf->sjcd", gate_grad, gate_weight, preferred_element_type=jnp.float32
    )
    row_grads = row_grads + jnp.einsum(
        "sjcf,jdf->sjcd", up_grad, up_weight, preferred_element_type=jnp.float32
    )
    row_grads = row_grads.astype(jnp.bfloat16).reshape(
        group_count, local_count * slot_cap, model_width
    )
    returned = lax.all_to_all(row_grads, "expert", split_axis=0, concat_axis=0, tiled=True).reshape(
        slot_total, model_width
    )
    returned = jnp.concatenate([returned, jnp.zeros((1, model_width), jnp.bfloat16)], 0)
    token_grads = jnp.sum(
        returned[target].reshape(tok_count, route_top, model_width).astype(jnp.float32), axis=1
    ).astype(jnp.bfloat16)
    dy_proj = jnp.einsum(
        "sjcd,dr->sjcr", dy_rows, projector, preferred_element_type=jnp.float32
    ).astype(jnp.bfloat16)
    partial_grads = jnp.stack(
        [
            jnp.einsum("sjcf,sjcr->jfr", gate_grad, x_proj, preferred_element_type=jnp.float32),
            jnp.einsum("sjcf,sjcr->jfr", up_grad, x_proj, preferred_element_type=jnp.float32),
            jnp.einsum("sjcf,sjcr->jfr", hidden, dy_proj, preferred_element_type=jnp.float32),
        ],
        1,
    )
    projected_grads = lax.psum(partial_grads, "replica")
    grads_low = projected_grads.astype(jnp.bfloat16)
    mixed = jnp.einsum(
        "sjcf,jfr->sjcr", gate_grad, grads_low[:, 0], preferred_element_type=jnp.float32
    )
    mixed = (
        mixed
        + jnp.einsum("sjcf,jfr->sjcr", up_grad, grads_low[:, 1], preferred_element_type=jnp.float32)
    ).astype(jnp.bfloat16)
    down_mix = jnp.einsum(
        "sjcf,jfr->sjcr", hidden, grads_low[:, 2], preferred_element_type=jnp.float32
    ).astype(jnp.bfloat16)
    power = jnp.einsum("sjcd,sjcr->dr", x_rows, mixed, preferred_element_type=jnp.float32)
    power = power + jnp.einsum(
        "sjcd,sjcr->dr", dy_rows, down_mix, preferred_element_type=jnp.float32
    )
    panel_rows = model_width // group_count
    power_sum = lax.psum(power, ("expert", "replica"))
    gram_total = jnp.dot(
        power_sum.T, power_sum, precision=lax.Precision.HIGHEST, preferred_element_type=jnp.float32
    )
    own_panel = lax.dynamic_slice_in_dim(
        power_sum, lax.axis_index("expert") * panel_rows, panel_rows, 0
    )
    lower = jnp.linalg.cholesky(gram_total)
    new_basis = (
        math.sqrt(model_width) * jax.scipy.linalg.solve_triangular(lower, own_panel.T, lower=True).T
    )
    return (token_grads, projected_grads, new_basis)


def power_of_two(count):
    return count > 1 and count & (count - 1) == 0


def body(*args):
    tok_count, local_count = args[0].shape[0], args[6].shape[0]
    groups, replicas = lax.axis_size("expert"), lax.axis_size("replica")
    slot_cap = tok_count * args[3].shape[1] // (local_count * groups)
    if (
        local_count * slot_cap >= tok_count
        and power_of_two(groups)
        and groups > 2
        and replicas == 4
        and args[9].shape[0] % 64 == 0
        and args[9].shape[1] % (32 * groups) == 0
    ):
        return gathered_body(*args)
    return routed_body(*args)


def solution(mesh):
    return jax.shard_map(
        body,
        mesh=mesh,
        in_specs=(
            P(("expert", "replica"), None),
            P(("expert", "replica"), None),
            P(("expert", "replica"), None),
            P(("expert", "replica"), None),
            P(("expert", "replica"), None),
            P(("expert", "replica"), None),
            P("expert", None, None),
            P("expert", None, None),
            P("expert", None, None),
            P("expert", None),
        ),
        out_specs=(
            P(("expert", "replica"), None),
            P("expert", None, None, None),
            P("expert", None),
        ),
        check_vma=False,
    )
```

```python
import functools
import math

import jax
import jax.numpy as jnp
from jax import lax
from jax.experimental import pallas as pl
from jax.experimental.pallas import tpu as pltpu
from jax.sharding import PartitionSpec as P

F32 = jnp.float32
BF16 = jnp.bfloat16
HIGH = lax.Precision.HIGHEST


MESH = pl.DeviceIdType.MESH


def solve_rows(block, scale, out_ref, a_ref, y_ref):
    n = a_ref.shape[0]
    rows = lax.broadcasted_iota(jnp.int32, (block, 1), 0)
    eye = (
        lax.broadcasted_iota(jnp.int32, (block, block), 0)
        == lax.broadcasted_iota(jnp.int32, (block, block), 1)
    ).astype(F32)
    for step in range(n // block):
        own = pl.ds(step * block, block)
        work = jnp.concatenate([a_ref[own, step * block : (step + 1) * block], eye], 1)
        pivots = jnp.ones((block, 1), F32)
        for k in range(0, block, 2):
            upper_row, lower_row = work[k : k + 1, :], work[k + 1 : k + 2, :]
            left, right = work[:, k : k + 1], work[:, k + 1 : k + 2]
            first_pivot = work[k : k + 1, k : k + 1]
            corner = work[k : k + 1, k + 1 : k + 2]
            first_inverse = 1.0 / first_pivot
            factor = corner * first_inverse
            second_pivot = work[k + 1 : k + 2, k + 1 : k + 2] - factor * corner
            pivots = jnp.where(rows == k, first_pivot, pivots)
            pivots = jnp.where(rows == k + 1, second_pivot, pivots)
            next_row = (lower_row - factor * upper_row) * (1.0 / second_pivot)
            next_column = jnp.where(rows > k + 1, right - left * factor, 0.0)
            column = jnp.where(rows > k, left, 0.0)
            work = work - column * (upper_row * first_inverse) - next_column * next_row
        inverse = work[:, block:] * (1.0 / jnp.sqrt(pivots))
        solved = jnp.dot(inverse, y_ref[own, :], precision=HIGH, preferred_element_type=F32)
        y_ref[own, :] = solved
        first = (step + 1) * block
        if first < n:
            upper = jnp.dot(
                inverse, a_ref[own, :], precision=HIGH, preferred_element_type=F32
            )
            lower = upper.T[first:, :]
            a_ref[first:, :] = a_ref[first:, :] - jnp.dot(
                lower, upper, precision=HIGH, preferred_element_type=F32
            )
            y_ref[first:, :] = y_ref[first:, :] - jnp.dot(
                lower, solved, precision=HIGH, preferred_element_type=F32
            )
    out_ref[...] = scale * y_ref[...].T


def greet(expert_peers, replica_peers):
    barrier = pltpu.get_barrier_semaphore()
    for peer in expert_peers:
        pl.semaphore_signal(barrier, inc=1, device_id={"expert": peer}, device_id_type=MESH)
    for peer in replica_peers:
        pl.semaphore_signal(barrier, inc=1, device_id={"replica": peer}, device_id_type=MESH)
    pl.semaphore_wait(barrier, len(expert_peers) + len(replica_peers))


def line_peer(me, outer, inner, step):
    return lax.rem(me // inner + step + outer, outer) * inner + lax.rem(me, inner)


def gather_kernel(
    groups,
    chunks,
    tok_ref,
    cot_ref,
    route_ref,
    basis_ref,
    tok_out,
    cot_out,
    route_out,
    basis_out,
    send_sem,
    recv_sem,
    own_sem,
):
    inner = 2
    outer = groups // inner
    me = lax.axis_index("expert")
    ahead = [line_peer(me, outer, inner, d) for d in range(outer)]
    behind = [line_peer(me, outer, inner, -d) for d in range(outer)]
    side = me + 1 - 2 * lax.rem(me, inner)
    greet(ahead[1:] + [side], [])

    own = [
        pltpu.make_async_copy(src, dst.at[me], own_sem.at[i])
        for i, (src, dst) in enumerate(
            (
                (tok_ref, tok_out),
                (cot_ref, cot_out),
                (route_ref, route_out),
                (basis_ref, basis_out),
            )
        )
    ]
    rows = tok_ref.shape[0] // chunks
    parts = [(route_ref, route_out, None)]
    parts += [(tok_ref, tok_out, pl.ds(c * rows, rows)) for c in range(chunks)]
    parts += [(basis_ref, basis_out, None)]
    parts += [(cot_ref, cot_out, pl.ds(c * rows, rows)) for c in range(chunks)]

    def copy(i, lane, source, target):
        src, dst, span = parts[i]
        if source is None:
            here = src if span is None else src.at[span]
            row = me
        else:
            here = dst.at[source] if span is None else dst.at[source, span]
            row = source
        there = dst.at[row] if span is None else dst.at[row, span]
        return pltpu.make_async_remote_copy(
            src_ref=here,
            dst_ref=there,
            send_sem=send_sem.at[i, lane],
            recv_sem=recv_sem.at[i, lane],
            device_id={"expert": target},
            device_id_type=MESH,
        )

    started = []

    def relay(i):
        for d in range(1, outer):
            line[i][d - 1].wait_recv()
            onward = copy(i, outer - 1 + d, behind[d], side)
            onward.start()
            started.append(onward)

    line = []
    flips = []
    for i in range(len(parts)):
        flips.append(copy(i, outer - 1, None, side))
        flips[-1].start()
        line.append([copy(i, d - 1, None, ahead[d]) for d in range(1, outer)])
        for c in line[-1]:
            c.start()
        if i >= 1:
            relay(i - 1)
        if i == 0:
            for c in own:
                c.start()
    relay(len(parts) - 1)
    for c in own:
        c.wait()
    for i in range(len(parts)):
        for c in line[i]:
            c.wait_send()
    for c in flips + started:
        c.wait()


def gather_all(tokens, cotangent, routes, basis):
    groups = lax.axis_size("expert")
    chunks = 8 if tokens.shape[0] % 128 == 0 else 1
    vmem = pl.BlockSpec(memory_space=pltpu.VMEM)
    arrays = (tokens, cotangent, routes, basis)
    count = 2 + 2 * chunks
    lanes = groups - 1
    return pl.pallas_call(
        functools.partial(gather_kernel, groups, chunks),
        out_shape=[jax.ShapeDtypeStruct((groups,) + a.shape, a.dtype) for a in arrays],
        in_specs=[vmem] * 4,
        out_specs=[pl.BlockSpec(memory_space=pl.ANY)] * 4,
        scratch_shapes=[
            pltpu.SemaphoreType.DMA((count, lanes)),
            pltpu.SemaphoreType.DMA((count, lanes)),
            pltpu.SemaphoreType.DMA((4,)),
        ],
        compiler_params=pltpu.CompilerParams(collective_id=0, has_side_effects=True),
    )(*arrays)


def sum_kernel(
    first_ref,
    second_ref,
    third_ref,
    out_ref,
    low_ref,
    half_in,
    low_out,
    low_in,
    send_sem,
    recv_sem,
):
    replica = lax.axis_index("replica")
    core = lax.rem(replica, 2)
    twin = replica + 1 - 2 * core
    across = replica + 2 - 4 * (replica // 2)
    greet([], [twin, across])
    parts = (first_ref, second_ref, third_ref)

    def send(src, dst, stage, i, target):
        return pltpu.make_async_remote_copy(
            src_ref=src,
            dst_ref=dst,
            send_sem=send_sem.at[stage, i],
            recv_sem=recv_sem.at[stage, i],
            device_id={"replica": target},
            device_id_type=MESH,
        )

    given = [send(p.at[1 - core], half_in.at[i], 0, i, twin) for i, p in enumerate(parts)]
    for c in given:
        c.start()
    crossed = []
    for i, p in enumerate(parts):
        given[i].wait()
        low_out[i] = (p[core] + half_in[i]).astype(BF16)
        crossed.append(send(low_out.at[i], low_in.at[i], 1, i, across))
        crossed[-1].start()
    joined = []
    for i in range(len(parts)):
        crossed[i].wait()
        out_ref[i, core] = low_out[i].astype(F32) + low_in[i].astype(F32)
        joined.append(send(out_ref.at[i, core], out_ref.at[i, core], 2, i, twin))
        joined[-1].start()
    for i in range(len(parts)):
        joined[i].wait()
        low_ref[i] = out_ref[i].astype(BF16)


def replica_sum(parts):
    rows, rank = parts[0].shape[1:]
    count = len(parts)
    vmem = pl.BlockSpec(memory_space=pltpu.VMEM)
    return pl.pallas_call(
        sum_kernel,
        out_shape=[
            jax.ShapeDtypeStruct((count, 2, rows, rank), F32),
            jax.ShapeDtypeStruct((count, 2, rows, rank), BF16),
        ],
        in_specs=[vmem] * count,
        out_specs=[vmem] * 2,
        scratch_shapes=[
            pltpu.VMEM((count, rows, rank), F32),
            pltpu.VMEM((count, rows, rank), BF16),
            pltpu.VMEM((count, rows, rank), BF16),
            pltpu.SemaphoreType.DMA((3, count)),
            pltpu.SemaphoreType.DMA((3, count)),
        ],
        compiler_params=pltpu.CompilerParams(collective_id=2, has_side_effects=True),
        cost_estimate=pl.CostEstimate(
            flops=30_000_000_000, bytes_accessed=100_000_000, transcendentals=0
        ),
    )(*parts)


def finish_kernel(
    groups,
    scale,
    power_ref,
    out_ref,
    half_in,
    half_sum,
    low_out,
    low_in,
    own_sum,
    side_out,
    side_in,
    pair_sum,
    line_out,
    line_in,
    panel_ref,
    gram_part,
    gram_in,
    gram_ref,
    a_ref,
    y_ref,
    send_sem,
    recv_sem,
    gather_send,
    gather_recv,
):
    inner = 2
    outer = groups // inner
    me = lax.axis_index("expert")
    replica = lax.axis_index("replica")
    core = lax.rem(replica, 2)
    row = replica // 2
    twin = replica + 1 - 2 * core
    across = replica + 2 - 4 * row
    place = lax.rem(me, inner)
    depth = me // inner
    side = me + 1 - 2 * place
    peers = [lax.rem(me + d, groups) for d in range(groups)]
    greet(peers[1:], [twin, across])
    rows, rank = power_ref.shape[3:]

    def send(src, dst, sem, target):
        return pltpu.make_async_remote_copy(
            src_ref=src,
            dst_ref=dst,
            send_sem=send_sem.at[sem],
            recv_sem=recv_sem.at[sem],
            device_id=target,
            device_id_type=MESH,
        )

    step = send(power_ref.at[:, 1 - core], half_in, 0, {"replica": twin})
    step.start()
    step.wait()
    half_sum[...] = power_ref[:, core] + half_in[...]
    low_out[...] = half_sum[:, 1 - row].astype(BF16)
    step = send(low_out, low_in, 1, {"replica": across})
    step.start()
    step.wait()
    own_sum[...] = half_sum[:, row] + low_in[...].astype(F32)
    for z in range(outer):
        side_out[z] = own_sum[z * inner + 1 - place].astype(BF16)
    step = send(side_out, side_in, 2, {"expert": side})
    step.start()
    step.wait()
    for z in range(outer):
        pair_sum[z] = own_sum[z * inner + place] + side_in[z].astype(F32)
    line_out[...] = pair_sum[...].astype(BF16)
    steps = []
    for d in range(1, outer):
        target = lax.rem(depth + d, outer)
        steps.append(
            send(
                line_out.at[target],
                line_in.at[d - 1],
                2 + d,
                {"expert": target * inner + place},
            )
        )
    for step in steps:
        step.start()
    for step in steps:
        step.wait()
    total = pair_sum[depth]
    for d in range(1, outer):
        total = total + line_in[d - 1].astype(F32)
    panel_ref[core, row] = total
    step = send(
        panel_ref.at[core, row], panel_ref.at[core, row], 2 + outer, {"replica": across}
    )
    step.start()
    step.wait()
    step = send(panel_ref.at[core], panel_ref.at[core], 3 + outer, {"replica": twin})
    step.start()
    step.wait()
    panel = panel_ref[...].reshape(4 * rows, rank)
    wide = rank // 4
    y_ref[...] = panel.T
    quarter = core * 2 + row
    part = jnp.dot(
        y_ref[pl.ds(pl.multiple_of(quarter * wide, wide), wide), :],
        panel,
        precision=HIGH,
        preferred_element_type=F32,
    )
    thin = wide // groups
    gram_part[...] = part.reshape(groups, thin, rank)

    def spread(src, dst, stage, d):
        return pltpu.make_async_remote_copy(
            src_ref=src,
            dst_ref=dst,
            send_sem=gather_send.at[stage, d - 1],
            recv_sem=gather_recv.at[stage, d - 1],
            device_id={"expert": peers[d]},
            device_id_type=MESH,
        )

    steps = [
        spread(gram_part.at[peers[d]], gram_in.at[d - 1], 0, d) for d in range(1, groups)
    ]
    for step in steps:
        step.start()
    for step in steps:
        step.wait()
    whole = gram_part[me]
    for d in range(1, groups):
        whole = whole + gram_in[d - 1]
    gram_ref[core, row, me] = whole
    mine = gram_ref.at[core, row, me]
    steps = [spread(mine, mine, 1, d) for d in range(1, groups)]
    for step in steps:
        step.start()
    for step in steps:
        step.wait()
    mine = gram_ref.at[core, row]
    step = send(mine, mine, 4 + outer, {"replica": across})
    step.start()
    step.wait()
    mine = gram_ref.at[core]
    step = send(mine, mine, 5 + outer, {"replica": twin})
    step.start()
    step.wait()
    a_ref[...] = gram_ref[...].reshape(rank, rank)
    solve_rows(64, scale, out_ref, a_ref, y_ref)


def finish(power, groups, scale):
    width, rank = power.shape
    rows = width // groups // 4
    outer = groups // 2
    vmem = pl.BlockSpec(memory_space=pltpu.VMEM)
    wide = rank // 4
    return pl.pallas_call(
        functools.partial(finish_kernel, groups, scale),
        out_shape=jax.ShapeDtypeStruct((4 * rows, rank), F32),
        in_specs=[vmem],
        out_specs=vmem,
        scratch_shapes=[
            pltpu.VMEM((groups, 2, rows, rank), F32),
            pltpu.VMEM((groups, 2, rows, rank), F32),
            pltpu.VMEM((groups, rows, rank), BF16),
            pltpu.VMEM((groups, rows, rank), BF16),
            pltpu.VMEM((groups, rows, rank), F32),
            pltpu.VMEM((outer, rows, rank), BF16),
            pltpu.VMEM((outer, rows, rank), BF16),
            pltpu.VMEM((outer, rows, rank), F32),
            pltpu.VMEM((outer, rows, rank), BF16),
            pltpu.VMEM((outer - 1, rows, rank), BF16),
            pltpu.VMEM((2, 2, rows, rank), F32),
            pltpu.VMEM((groups, wide // groups, rank), F32),
            pltpu.VMEM((groups - 1, wide // groups, rank), F32),
            pltpu.VMEM((2, 2, groups, wide // groups, rank), F32),
            pltpu.VMEM((rank, rank), F32),
            pltpu.VMEM((rank, 4 * rows), F32),
            pltpu.SemaphoreType.DMA((6 + outer,)),
            pltpu.SemaphoreType.DMA((6 + outer,)),
            pltpu.SemaphoreType.DMA((2, groups - 1)),
            pltpu.SemaphoreType.DMA((2, groups - 1)),
        ],
        compiler_params=pltpu.CompilerParams(collective_id=1, has_side_effects=True),
        cost_estimate=pl.CostEstimate(
            flops=40_000_000_000, bytes_accessed=100_000_000, transcendentals=0
        ),
    )(power.reshape(groups, 2, 2, rows, rank))


def gathered_body(
    tokens,
    cotangent,
    route_weights,
    expert_ids,
    slot_ids,
    kept_mask,
    gate_weight,
    up_weight,
    down_weight,
    projector_basis,
):
    tok_count, width = tokens.shape
    local_count = gate_weight.shape[0]
    groups = lax.axis_size("expert")
    expert_total = local_count * groups
    slot_cap = tok_count * expert_ids.shape[1] // expert_total
    inner = 2
    outer = groups // inner
    me = lax.axis_index("expert")

    def shift(value, step):
        perm = [
            (e, ((e // inner + step) % outer) * inner + e % inner) for e in range(groups)
        ]
        return lax.ppermute(value, "expert", perm)

    def flip(value):
        return lax.ppermute(value, "expert", [(e, e ^ 1) for e in range(groups)])

    match = (expert_ids[None] == jnp.arange(expert_total)[:, None, None]) & (kept_mask[None] > 0)
    slot_map = jnp.max(jnp.where(match, slot_ids[None], -1), -1).astype(F32)
    weight_map = jnp.sum(jnp.where(match, route_weights[None], 0.0), -1)
    x_blocks, dy_blocks, routes, projector = gather_all(
        tokens,
        cotangent,
        jnp.concatenate([slot_map, weight_map], 0),
        (projector_basis * (1.0 / math.sqrt(width))).astype(BF16),
    )
    projector = projector.reshape(width, -1)
    mine = me * local_count
    slots = lax.dynamic_slice_in_dim(routes, mine, local_count, 1).astype(jnp.int32)
    weights = lax.dynamic_slice_in_dim(routes, expert_total + mine, local_count, 1)
    taken = slots[:, :, None, :] == jnp.arange(slot_cap)[None, None, :, None]
    select = taken.astype(BF16)
    slot_weight = jnp.sum(jnp.where(taken, weights[:, :, None, :], 0.0), -1)

    def dot(spec, a, b):
        return jnp.einsum(spec, a, b, preferred_element_type=F32)

    x_rows = dot("sjct,std->jscd", select, x_blocks).astype(BF16)
    x_rows = x_rows.reshape(local_count, -1, width)
    gate = dot("jpd,jdf->jpf", x_rows, gate_weight)
    upper = dot("jpd,jdf->jpf", x_rows, up_weight)
    sigma = jax.nn.sigmoid(gate)
    activated = gate * sigma
    slope = sigma * (1.0 + gate * (1.0 - sigma))
    hidden = (activated * upper).astype(BF16)
    x_proj = dot("jpd,dr->jpr", x_rows, projector).astype(BF16)

    dy_rows = dot("sjct,std->jscd", select, dy_blocks)
    dy_rows = (dy_rows * slot_weight.transpose(1, 0, 2)[..., None]).astype(BF16)
    dy_rows = dy_rows.reshape(local_count, -1, width)
    hidden_grad = dot("jpd,jfd->jpf", dy_rows, down_weight)
    up_grad = (hidden_grad * activated).astype(BF16)
    gate_grad = (hidden_grad * upper * slope).astype(BF16)
    dy_proj = dot("jpd,dr->jpr", dy_rows, projector).astype(BF16)

    row_grads = dot("jpf,jdf->jpd", gate_grad, gate_weight) + dot(
        "jpf,jdf->jpd", up_grad, up_weight
    )
    row_grads = row_grads.astype(BF16).reshape(local_count, groups, slot_cap, width)
    back = dot("sjct,jscd->std", select, row_grads).astype(BF16)
    back = back.reshape(outer, inner, tok_count, width)
    place, depth = me % inner, me // inner
    stay, leave = [], []
    for d in range(outer):
        pair = lax.dynamic_index_in_dim(back, (depth + d) % outer, 0, False)
        stay.append(lax.dynamic_index_in_dim(pair, place, 0, False))
        leave.append(lax.dynamic_index_in_dim(pair, 1 - place, 0, False))
    leave, gate_grad, up_grad, hidden = lax.optimization_barrier(
        (leave, gate_grad, up_grad, hidden)
    )
    arrived = [flip(v) for v in leave]

    ff = gate_grad.shape[-1]
    partial = [
        dot("jpf,jpr->jfr", gate_grad, x_proj),
        dot("jpf,jpr->jfr", up_grad, x_proj),
        dot("jpf,jpr->jfr", hidden, dy_proj),
    ]
    rank = x_proj.shape[-1]
    grads, grads_low = replica_sum([p.reshape(2, -1, rank) for p in partial])
    projected_grads = grads.reshape(3, local_count, ff, rank).transpose(1, 0, 2, 3)
    grads_low = grads_low.reshape(3, local_count, ff, rank)

    mixed = dot("jpf,jfr->jpr", gate_grad, grads_low[0])
    mixed = (mixed + dot("jpf,jfr->jpr", up_grad, grads_low[1])).astype(BF16)
    down_mix = dot("jpf,jfr->jpr", hidden, grads_low[2]).astype(BF16)
    power = dot("jpd,jpr->dr", x_rows, mixed) + dot("jpd,jpr->dr", dy_rows, down_mix)

    pairs = [a.astype(F32) + b.astype(F32) for a, b in zip(stay, arrived)]
    sent = [p.astype(BF16) for p in pairs[1:]]
    sent, power = lax.optimization_barrier((sent, power))
    new_basis = finish(power, groups, math.sqrt(width))
    total = pairs[0]
    for d in range(1, outer):
        total = total + shift(sent[d - 1], d).astype(F32)
    token_grads = total.astype(BF16)
    return (token_grads, projected_grads, new_basis)


def routed_body(
    tokens,
    cotangent,
    route_weights,
    expert_ids,
    slot_ids,
    kept_mask,
    gate_weight,
    up_weight,
    down_weight,
    projector_basis,
):
    tok_count, model_width = tokens.shape
    route_top = expert_ids.shape[1]
    local_count = gate_weight.shape[0]
    group_count = lax.axis_size("expert")
    expert_total = local_count * group_count
    slot_cap = tok_count * route_top // expert_total
    slot_total = expert_total * slot_cap
    route_count = tok_count * route_top
    target = jnp.where(kept_mask > 0, expert_ids * slot_cap + slot_ids, slot_total).reshape(-1)
    table = (
        jnp.full((slot_total,), route_count, jnp.int32)
        .at[target]
        .set(jnp.arange(route_count, dtype=jnp.int32), mode="drop")
    )
    owner = table // route_top
    tokens_pad = jnp.concatenate([tokens, jnp.zeros((1, model_width), tokens.dtype)], 0)
    cotangent_pad = jnp.concatenate([cotangent, jnp.zeros((1, model_width), cotangent.dtype)], 0)
    weight_pad = jnp.concatenate([route_weights.reshape(-1), jnp.zeros((1,), jnp.float32)], 0)
    x_send = tokens_pad[owner].reshape(group_count, local_count * slot_cap, model_width)
    dy_send = (cotangent_pad[owner].astype(jnp.float32) * weight_pad[table][:, None]).astype(
        jnp.bfloat16
    )
    dy_send = dy_send.reshape(group_count, local_count * slot_cap, model_width)
    full_basis = lax.all_gather(
        projector_basis.astype(jnp.bfloat16), "expert", axis=0, tiled=True
    ).astype(projector_basis.dtype)
    projector = (full_basis * (1.0 / math.sqrt(model_width))).astype(jnp.bfloat16)
    block_shape = (group_count, local_count, slot_cap, model_width)
    x_recv, dy_recv = (
        lax.all_to_all(x_send, "expert", split_axis=0, concat_axis=0, tiled=True),
        lax.all_to_all(dy_send, "expert", split_axis=0, concat_axis=0, tiled=True),
    )
    x_rows = x_recv.reshape(block_shape)
    gate = jnp.einsum("sjcd,jdf->sjcf", x_rows, gate_weight, preferred_element_type=jnp.float32)
    upper = jnp.einsum("sjcd,jdf->sjcf", x_rows, up_weight, preferred_element_type=jnp.float32)
    sigma = jax.nn.sigmoid(gate)
    activated = gate * sigma
    slope = sigma * (1.0 + gate * (1.0 - sigma))
    hidden = (activated * upper).astype(jnp.bfloat16)
    x_proj = jnp.einsum(
        "sjcd,dr->sjcr", x_rows, projector, preferred_element_type=jnp.float32
    ).astype(jnp.bfloat16)
    x_rows, upper, activated, slope, hidden, x_proj = (
        x_rows,
        upper,
        activated,
        slope,
        hidden,
        x_proj,
    )
    dy_rows = dy_recv.reshape(block_shape)
    hidden_grad = jnp.einsum(
        "sjcd,jfd->sjcf", dy_rows, down_weight, preferred_element_type=jnp.float32
    )
    up_grad = (hidden_grad * activated).astype(jnp.bfloat16)
    gate_grad = (hidden_grad * upper * slope).astype(jnp.bfloat16)
    row_grads = jnp.einsum(
        "sjcf,jdf->sjcd", gate_grad, gate_weight, preferred_element_type=jnp.float32
    )
    row_grads = row_grads + jnp.einsum(
        "sjcf,jdf->sjcd", up_grad, up_weight, preferred_element_type=jnp.float32
    )
    row_grads = row_grads.astype(jnp.bfloat16).reshape(
        group_count, local_count * slot_cap, model_width
    )
    returned = lax.all_to_all(row_grads, "expert", split_axis=0, concat_axis=0, tiled=True).reshape(
        slot_total, model_width
    )
    returned = jnp.concatenate([returned, jnp.zeros((1, model_width), jnp.bfloat16)], 0)
    token_grads = jnp.sum(
        returned[target].reshape(tok_count, route_top, model_width).astype(jnp.float32), axis=1
    ).astype(jnp.bfloat16)
    dy_proj = jnp.einsum(
        "sjcd,dr->sjcr", dy_rows, projector, preferred_element_type=jnp.float32
    ).astype(jnp.bfloat16)
    partial_grads = jnp.stack(
        [
            jnp.einsum("sjcf,sjcr->jfr", gate_grad, x_proj, preferred_element_type=jnp.float32),
            jnp.einsum("sjcf,sjcr->jfr", up_grad, x_proj, preferred_element_type=jnp.float32),
            jnp.einsum("sjcf,sjcr->jfr", hidden, dy_proj, preferred_element_type=jnp.float32),
        ],
        1,
    )
    projected_grads = lax.psum(partial_grads, "replica")
    grads_low = projected_grads.astype(jnp.bfloat16)
    mixed = jnp.einsum(
        "sjcf,jfr->sjcr", gate_grad, grads_low[:, 0], preferred_element_type=jnp.float32
    )
    mixed = (
        mixed
        + jnp.einsum("sjcf,jfr->sjcr", up_grad, grads_low[:, 1], preferred_element_type=jnp.float32)
    ).astype(jnp.bfloat16)
    down_mix = jnp.einsum(
        "sjcf,jfr->sjcr", hidden, grads_low[:, 2], preferred_element_type=jnp.float32
    ).astype(jnp.bfloat16)
    power = jnp.einsum("sjcd,sjcr->dr", x_rows, mixed, preferred_element_type=jnp.float32)
    power = power + jnp.einsum(
        "sjcd,sjcr->dr", dy_rows, down_mix, preferred_element_type=jnp.float32
    )
    panel_rows = model_width // group_count
    power_sum = lax.psum(power, ("expert", "replica"))
    gram_total = jnp.dot(
        power_sum.T, power_sum, precision=lax.Precision.HIGHEST, preferred_element_type=jnp.float32
    )
    own_panel = lax.dynamic_slice_in_dim(
        power_sum, lax.axis_index("expert") * panel_rows, panel_rows, 0
    )
    lower = jnp.linalg.cholesky(gram_total)
    new_basis = (
        math.sqrt(model_width) * jax.scipy.linalg.solve_triangular(lower, own_panel.T, lower=True).T
    )
    return (token_grads, projected_grads, new_basis)


def power_of_two(count):
    return count > 1 and count & (count - 1) == 0


def body(*args):
    tok_count, local_count = args[0].shape[0], args[6].shape[0]
    groups, replicas = lax.axis_size("expert"), lax.axis_size("replica")
    slot_cap = tok_count * args[3].shape[1] // (local_count * groups)
    if (
        local_count * slot_cap >= tok_count
        and power_of_two(groups)
        and groups > 2
        and local_count * args[6].shape[2] % 32 == 0
        and replicas == 4
        and args[9].shape[0] % 64 == 0
        and args[9].shape[1] % (32 * groups) == 0
    ):
        return gathered_body(*args)
    return routed_body(*args)


def solution(mesh):
    return jax.shard_map(
        body,
        mesh=mesh,
        in_specs=(
            P(("expert", "replica"), None),
            P(("expert", "replica"), None),
            P(("expert", "replica"), None),
            P(("expert", "replica"), None),
            P(("expert", "replica"), None),
            P(("expert", "replica"), None),
            P("expert", None, None),
            P("expert", None, None),
            P("expert", None, None),
            P("expert", None),
        ),
        out_specs=(
            P(("expert", "replica"), None),
            P("expert", None, None, None),
            P("expert", None),
        ),
        check_vma=False,
    )
```

```python
import functools
import math

import jax
import jax.numpy as jnp
from jax import lax
from jax.experimental import pallas as pl
from jax.experimental.pallas import tpu as pltpu
from jax.sharding import PartitionSpec as P

F32 = jnp.float32
BF16 = jnp.bfloat16
HIGH = lax.Precision.HIGHEST


MESH = pl.DeviceIdType.MESH
TILE = 8


def solve_rows(block, scale, out_ref, a_ref, y_ref):
    n = a_ref.shape[0]
    rows = lax.broadcasted_iota(jnp.int32, (block, 1), 0)
    eye = (
        lax.broadcasted_iota(jnp.int32, (block, block), 0)
        == lax.broadcasted_iota(jnp.int32, (block, block), 1)
    ).astype(F32)
    for step in range(n // block):
        own = pl.ds(step * block, block)
        work = jnp.concatenate([a_ref[own, step * block : (step + 1) * block], eye], 1)
        done, tail = [], work
        for k in range(block):
            at = k % TILE
            column = jnp.broadcast_to(tail[:, k : k + 1], tail.shape)
            row = tail[at : at + 1, :] * (1.0 / column[at : at + 1, :])
            below = rows[: tail.shape[0]] > at
            tail = tail - jnp.where(below, column, 0.0) * row
            if at == TILE - 1:
                done.append(tail[:TILE])
                tail = tail[TILE:]
        work = jnp.concatenate(done, 0)
        pivots = jnp.sum(work[:, :block] * eye, 1, keepdims=True)
        inverse = work[:, block:] * (1.0 / jnp.sqrt(pivots))
        solved = jnp.dot(inverse, y_ref[own, :], precision=HIGH, preferred_element_type=F32)
        y_ref[own, :] = solved
        first = (step + 1) * block
        if first < n:
            upper = jnp.dot(
                inverse, a_ref[own, :], precision=HIGH, preferred_element_type=F32
            )
            lower = upper.T[first:, :]
            a_ref[first:, :] = a_ref[first:, :] - jnp.dot(
                lower, upper, precision=HIGH, preferred_element_type=F32
            )
            y_ref[first:, :] = y_ref[first:, :] - jnp.dot(
                lower, solved, precision=HIGH, preferred_element_type=F32
            )
    out_ref[...] = scale * y_ref[...].T


def greet(expert_peers, replica_peers):
    barrier = pltpu.get_barrier_semaphore()
    for peer in expert_peers:
        pl.semaphore_signal(barrier, inc=1, device_id={"expert": peer}, device_id_type=MESH)
    for peer in replica_peers:
        pl.semaphore_signal(barrier, inc=1, device_id={"replica": peer}, device_id_type=MESH)
    pl.semaphore_wait(barrier, len(expert_peers) + len(replica_peers))


def line_peer(me, outer, inner, step):
    return lax.rem(me // inner + step + outer, outer) * inner + lax.rem(me, inner)


def gather_kernel(
    groups,
    chunks,
    tok_ref,
    cot_ref,
    route_ref,
    basis_ref,
    tok_out,
    cot_out,
    route_out,
    basis_out,
    send_sem,
    recv_sem,
    own_sem,
):
    inner = 2
    outer = groups // inner
    me = lax.axis_index("expert")
    ahead = [line_peer(me, outer, inner, d) for d in range(outer)]
    behind = [line_peer(me, outer, inner, -d) for d in range(outer)]
    side = me + 1 - 2 * lax.rem(me, inner)
    greet(ahead[1:] + [side], [])

    own = [
        pltpu.make_async_copy(src, dst.at[me], own_sem.at[i])
        for i, (src, dst) in enumerate(
            (
                (tok_ref, tok_out),
                (cot_ref, cot_out),
                (route_ref, route_out),
                (basis_ref, basis_out),
            )
        )
    ]
    rows = tok_ref.shape[0] // chunks
    parts = [(route_ref, route_out, None)]
    parts += [(tok_ref, tok_out, pl.ds(c * rows, rows)) for c in range(chunks)]
    parts += [(basis_ref, basis_out, None)]
    parts += [(cot_ref, cot_out, pl.ds(c * rows, rows)) for c in range(chunks)]

    def copy(i, lane, source, target):
        src, dst, span = parts[i]
        if source is None:
            here = src if span is None else src.at[span]
            row = me
        else:
            here = dst.at[source] if span is None else dst.at[source, span]
            row = source
        there = dst.at[row] if span is None else dst.at[row, span]
        return pltpu.make_async_remote_copy(
            src_ref=here,
            dst_ref=there,
            send_sem=send_sem.at[i, lane],
            recv_sem=recv_sem.at[i, lane],
            device_id={"expert": target},
            device_id_type=MESH,
        )

    started = []

    def relay(i):
        for d in range(1, outer):
            line[i][d - 1].wait_recv()
            onward = copy(i, outer - 1 + d, behind[d], side)
            onward.start()
            started.append(onward)

    line = []
    flips = []
    for i in range(len(parts)):
        flips.append(copy(i, outer - 1, None, side))
        flips[-1].start()
        line.append([copy(i, d - 1, None, ahead[d]) for d in range(1, outer)])
        for c in line[-1]:
            c.start()
        if i >= 1:
            relay(i - 1)
        if i == 0:
            for c in own:
                c.start()
    relay(len(parts) - 1)
    for c in own:
        c.wait()
    for i in range(len(parts)):
        for c in line[i]:
            c.wait_send()
    for c in flips + started:
        c.wait()


def gather_all(tokens, cotangent, routes, basis):
    groups = lax.axis_size("expert")
    chunks = 8 if tokens.shape[0] % 128 == 0 else 1
    vmem = pl.BlockSpec(memory_space=pltpu.VMEM)
    arrays = (tokens, cotangent, routes, basis)
    count = 2 + 2 * chunks
    lanes = groups - 1
    return pl.pallas_call(
        functools.partial(gather_kernel, groups, chunks),
        out_shape=[jax.ShapeDtypeStruct((groups,) + a.shape, a.dtype) for a in arrays],
        in_specs=[vmem] * 4,
        out_specs=[pl.BlockSpec(memory_space=pl.ANY)] * 4,
        scratch_shapes=[
            pltpu.SemaphoreType.DMA((count, lanes)),
            pltpu.SemaphoreType.DMA((count, lanes)),
            pltpu.SemaphoreType.DMA((4,)),
        ],
        compiler_params=pltpu.CompilerParams(collective_id=0, has_side_effects=True),
    )(*arrays)


def sum_kernel(
    first_ref,
    second_ref,
    third_ref,
    out_ref,
    low_ref,
    half_in,
    low_out,
    low_in,
    send_sem,
    recv_sem,
):
    replica = lax.axis_index("replica")
    core = lax.rem(replica, 2)
    twin = replica + 1 - 2 * core
    across = replica + 2 - 4 * (replica // 2)
    greet([], [twin, across])
    parts = (first_ref, second_ref, third_ref)

    def send(src, dst, stage, i, target):
        return pltpu.make_async_remote_copy(
            src_ref=src,
            dst_ref=dst,
            send_sem=send_sem.at[stage, i],
            recv_sem=recv_sem.at[stage, i],
            device_id={"replica": target},
            device_id_type=MESH,
        )

    given = [send(p.at[1 - core], half_in.at[i], 0, i, twin) for i, p in enumerate(parts)]
    for c in given:
        c.start()
    crossed = []
    for i, p in enumerate(parts):
        given[i].wait()
        low_out[i] = (p[core] + half_in[i]).astype(BF16)
        crossed.append(send(low_out.at[i], low_in.at[i], 1, i, across))
        crossed[-1].start()
    joined = []
    for i in range(len(parts)):
        crossed[i].wait()
        out_ref[i, core] = low_out[i].astype(F32) + low_in[i].astype(F32)
        joined.append(send(out_ref.at[i, core], out_ref.at[i, core], 2, i, twin))
        joined[-1].start()
    for i in range(len(parts)):
        joined[i].wait()
        low_ref[i] = out_ref[i].astype(BF16)


def replica_sum(parts):
    rows, rank = parts[0].shape[1:]
    count = len(parts)
    vmem = pl.BlockSpec(memory_space=pltpu.VMEM)
    return pl.pallas_call(
        sum_kernel,
        out_shape=[
            jax.ShapeDtypeStruct((count, 2, rows, rank), F32),
            jax.ShapeDtypeStruct((count, 2, rows, rank), BF16),
        ],
        in_specs=[vmem] * count,
        out_specs=[vmem] * 2,
        scratch_shapes=[
            pltpu.VMEM((count, rows, rank), F32),
            pltpu.VMEM((count, rows, rank), BF16),
            pltpu.VMEM((count, rows, rank), BF16),
            pltpu.SemaphoreType.DMA((3, count)),
            pltpu.SemaphoreType.DMA((3, count)),
        ],
        compiler_params=pltpu.CompilerParams(collective_id=2, has_side_effects=True),
        cost_estimate=pl.CostEstimate(
            flops=30_000_000_000, bytes_accessed=100_000_000, transcendentals=0
        ),
    )(*parts)


def finish_kernel(
    groups,
    scale,
    power_ref,
    out_ref,
    half_in,
    half_sum,
    low_out,
    low_in,
    own_sum,
    side_out,
    side_in,
    pair_sum,
    line_out,
    line_in,
    panel_ref,
    gram_part,
    gram_in,
    gram_ref,
    a_ref,
    y_ref,
    send_sem,
    recv_sem,
    gather_send,
    gather_recv,
):
    inner = 2
    outer = groups // inner
    me = lax.axis_index("expert")
    replica = lax.axis_index("replica")
    core = lax.rem(replica, 2)
    row = replica // 2
    twin = replica + 1 - 2 * core
    across = replica + 2 - 4 * row
    place = lax.rem(me, inner)
    depth = me // inner
    side = me + 1 - 2 * place
    peers = [lax.rem(me + d, groups) for d in range(groups)]
    greet(peers[1:], [twin, across])
    rows, rank = power_ref.shape[3:]

    def send(src, dst, sem, target):
        return pltpu.make_async_remote_copy(
            src_ref=src,
            dst_ref=dst,
            send_sem=send_sem.at[sem],
            recv_sem=recv_sem.at[sem],
            device_id=target,
            device_id_type=MESH,
        )

    step = send(power_ref.at[:, 1 - core], half_in, 0, {"replica": twin})
    step.start()
    step.wait()
    half_sum[...] = power_ref[:, core] + half_in[...]
    low_out[...] = half_sum[:, 1 - row].astype(BF16)
    step = send(low_out, low_in, 1, {"replica": across})
    step.start()
    step.wait()
    own_sum[...] = half_sum[:, row] + low_in[...].astype(F32)
    for z in range(outer):
        side_out[z] = own_sum[z * inner + 1 - place].astype(BF16)
    step = send(side_out, side_in, 2, {"expert": side})
    step.start()
    step.wait()
    for z in range(outer):
        pair_sum[z] = own_sum[z * inner + place] + side_in[z].astype(F32)
    line_out[...] = pair_sum[...].astype(BF16)
    steps = []
    for d in range(1, outer):
        target = lax.rem(depth + d, outer)
        steps.append(
            send(
                line_out.at[target],
                line_in.at[d - 1],
                2 + d,
                {"expert": target * inner + place},
            )
        )
    for step in steps:
        step.start()
    for step in steps:
        step.wait()
    total = pair_sum[depth]
    for d in range(1, outer):
        total = total + line_in[d - 1].astype(F32)
    panel_ref[core, row] = total
    step = send(
        panel_ref.at[core, row], panel_ref.at[core, row], 2 + outer, {"replica": across}
    )
    step.start()
    step.wait()
    step = send(panel_ref.at[core], panel_ref.at[core], 3 + outer, {"replica": twin})
    step.start()
    step.wait()
    panel = panel_ref[...].reshape(4 * rows, rank)
    wide = rank // 4
    y_ref[...] = panel.T
    quarter = core * 2 + row
    part = jnp.dot(
        y_ref[pl.ds(pl.multiple_of(quarter * wide, wide), wide), :],
        panel,
        precision=HIGH,
        preferred_element_type=F32,
    )
    thin = wide // groups
    gram_part[...] = part.reshape(groups, thin, rank)

    def spread(src, dst, stage, d):
        return pltpu.make_async_remote_copy(
            src_ref=src,
            dst_ref=dst,
            send_sem=gather_send.at[stage, d - 1],
            recv_sem=gather_recv.at[stage, d - 1],
            device_id={"expert": peers[d]},
            device_id_type=MESH,
        )

    steps = [
        spread(gram_part.at[peers[d]], gram_in.at[d - 1], 0, d) for d in range(1, groups)
    ]
    for step in steps:
        step.start()
    for step in steps:
        step.wait()
    whole = gram_part[me]
    for d in range(1, groups):
        whole = whole + gram_in[d - 1]
    gram_ref[core, row, me] = whole
    mine = gram_ref.at[core, row, me]
    steps = [spread(mine, mine, 1, d) for d in range(1, groups)]
    for step in steps:
        step.start()
    for step in steps:
        step.wait()
    mine = gram_ref.at[core, row]
    step = send(mine, mine, 4 + outer, {"replica": across})
    step.start()
    step.wait()
    mine = gram_ref.at[core]
    step = send(mine, mine, 5 + outer, {"replica": twin})
    step.start()
    step.wait()
    a_ref[...] = gram_ref[...].reshape(rank, rank)
    solve_rows(64, scale, out_ref, a_ref, y_ref)


def finish(power, groups, scale):
    width, rank = power.shape
    rows = width // groups // 4
    outer = groups // 2
    vmem = pl.BlockSpec(memory_space=pltpu.VMEM)
    wide = rank // 4
    return pl.pallas_call(
        functools.partial(finish_kernel, groups, scale),
        out_shape=jax.ShapeDtypeStruct((4 * rows, rank), F32),
        in_specs=[vmem],
        out_specs=vmem,
        scratch_shapes=[
            pltpu.VMEM((groups, 2, rows, rank), F32),
            pltpu.VMEM((groups, 2, rows, rank), F32),
            pltpu.VMEM((groups, rows, rank), BF16),
            pltpu.VMEM((groups, rows, rank), BF16),
            pltpu.VMEM((groups, rows, rank), F32),
            pltpu.VMEM((outer, rows, rank), BF16),
            pltpu.VMEM((outer, rows, rank), BF16),
            pltpu.VMEM((outer, rows, rank), F32),
            pltpu.VMEM((outer, rows, rank), BF16),
            pltpu.VMEM((outer - 1, rows, rank), BF16),
            pltpu.VMEM((2, 2, rows, rank), F32),
            pltpu.VMEM((groups, wide // groups, rank), F32),
            pltpu.VMEM((groups - 1, wide // groups, rank), F32),
            pltpu.VMEM((2, 2, groups, wide // groups, rank), F32),
            pltpu.VMEM((rank, rank), F32),
            pltpu.VMEM((rank, 4 * rows), F32),
            pltpu.SemaphoreType.DMA((6 + outer,)),
            pltpu.SemaphoreType.DMA((6 + outer,)),
            pltpu.SemaphoreType.DMA((2, groups - 1)),
            pltpu.SemaphoreType.DMA((2, groups - 1)),
        ],
        compiler_params=pltpu.CompilerParams(collective_id=1, has_side_effects=True),
        cost_estimate=pl.CostEstimate(
            flops=40_000_000_000, bytes_accessed=100_000_000, transcendentals=0
        ),
    )(power.reshape(groups, 2, 2, rows, rank))


def gathered_body(
    tokens,
    cotangent,
    route_weights,
    expert_ids,
    slot_ids,
    kept_mask,
    gate_weight,
    up_weight,
    down_weight,
    projector_basis,
):
    tok_count, width = tokens.shape
    local_count = gate_weight.shape[0]
    groups = lax.axis_size("expert")
    expert_total = local_count * groups
    slot_cap = tok_count * expert_ids.shape[1] // expert_total
    inner = 2
    outer = groups // inner
    me = lax.axis_index("expert")

    def shift(value, step):
        perm = [
            (e, ((e // inner + step) % outer) * inner + e % inner) for e in range(groups)
        ]
        return lax.ppermute(value, "expert", perm)

    def flip(value):
        return lax.ppermute(value, "expert", [(e, e ^ 1) for e in range(groups)])

    match = (expert_ids[None] == jnp.arange(expert_total)[:, None, None]) & (kept_mask[None] > 0)
    slot_map = jnp.max(jnp.where(match, slot_ids[None], -1), -1).astype(F32)
    weight_map = jnp.sum(jnp.where(match, route_weights[None], 0.0), -1)
    x_blocks, dy_blocks, routes, projector = gather_all(
        tokens,
        cotangent,
        jnp.concatenate([slot_map, weight_map], 0),
        (projector_basis * (1.0 / math.sqrt(width))).astype(BF16),
    )
    projector = projector.reshape(width, -1)
    mine = me * local_count
    slots = lax.dynamic_slice_in_dim(routes, mine, local_count, 1).astype(jnp.int32)
    weights = lax.dynamic_slice_in_dim(routes, expert_total + mine, local_count, 1)
    taken = slots[:, :, None, :] == jnp.arange(slot_cap)[None, None, :, None]
    select = taken.astype(BF16)
    slot_weight = jnp.sum(jnp.where(taken, weights[:, :, None, :], 0.0), -1)

    def dot(spec, a, b):
        return jnp.einsum(spec, a, b, preferred_element_type=F32)

    x_rows = dot("sjct,std->jscd", select, x_blocks).astype(BF16)
    x_rows = x_rows.reshape(local_count, -1, width)
    gate = dot("jpd,jdf->jpf", x_rows, gate_weight)
    upper = dot("jpd,jdf->jpf", x_rows, up_weight)
    sigma = jax.nn.sigmoid(gate)
    activated = gate * sigma
    slope = sigma * (1.0 + gate * (1.0 - sigma))
    hidden = (activated * upper).astype(BF16)
    x_proj = dot("jpd,dr->jpr", x_rows, projector).astype(BF16)

    dy_rows = dot("sjct,std->jscd", select, dy_blocks)
    dy_rows = (dy_rows * slot_weight.transpose(1, 0, 2)[..., None]).astype(BF16)
    dy_rows = dy_rows.reshape(local_count, -1, width)
    hidden_grad = dot("jpd,jfd->jpf", dy_rows, down_weight)
    up_grad = (hidden_grad * activated).astype(BF16)
    gate_grad = (hidden_grad * upper * slope).astype(BF16)
    dy_proj = dot("jpd,dr->jpr", dy_rows, projector).astype(BF16)

    row_grads = dot("jpf,jdf->jpd", gate_grad, gate_weight) + dot(
        "jpf,jdf->jpd", up_grad, up_weight
    )
    row_grads = row_grads.astype(BF16).reshape(local_count, groups, slot_cap, width)
    back = dot("sjct,jscd->std", select, row_grads).astype(BF16)
    back = back.reshape(outer, inner, tok_count, width)
    place, depth = me % inner, me // inner
    stay, leave = [], []
    for d in range(outer):
        pair = lax.dynamic_index_in_dim(back, (depth + d) % outer, 0, False)
        stay.append(lax.dynamic_index_in_dim(pair, place, 0, False))
        leave.append(lax.dynamic_index_in_dim(pair, 1 - place, 0, False))
    leave, gate_grad, up_grad, hidden = lax.optimization_barrier(
        (leave, gate_grad, up_grad, hidden)
    )
    arrived = [flip(v) for v in leave]

    ff = gate_grad.shape[-1]
    partial = [
        dot("jpf,jpr->jfr", gate_grad, x_proj),
        dot("jpf,jpr->jfr", up_grad, x_proj),
        dot("jpf,jpr->jfr", hidden, dy_proj),
    ]
    rank = x_proj.shape[-1]
    grads, grads_low = replica_sum([p.reshape(2, -1, rank) for p in partial])
    projected_grads = grads.reshape(3, local_count, ff, rank).transpose(1, 0, 2, 3)
    grads_low = grads_low.reshape(3, local_count, ff, rank)
    sent = [
        (a.astype(F32) + b.astype(F32)).astype(BF16)
        for a, b in zip(stay[1:], arrived[1:])
    ]
    sent, grads_low = lax.optimization_barrier((sent, grads_low))
    returned = [shift(v, d) for d, v in enumerate(sent, 1)]

    mixed = dot("jpf,jfr->jpr", gate_grad, grads_low[0])
    mixed = (mixed + dot("jpf,jfr->jpr", up_grad, grads_low[1])).astype(BF16)
    down_mix = dot("jpf,jfr->jpr", hidden, grads_low[2]).astype(BF16)
    power = dot("jpd,jpr->dr", x_rows, mixed) + dot("jpd,jpr->dr", dy_rows, down_mix)

    new_basis = finish(power, groups, math.sqrt(width))
    total = stay[0].astype(F32) + arrived[0].astype(F32)
    for value in returned:
        total = total + value.astype(F32)
    token_grads = total.astype(BF16)
    return (token_grads, projected_grads, new_basis)


def routed_body(
    tokens,
    cotangent,
    route_weights,
    expert_ids,
    slot_ids,
    kept_mask,
    gate_weight,
    up_weight,
    down_weight,
    projector_basis,
):
    tok_count, model_width = tokens.shape
    route_top = expert_ids.shape[1]
    local_count = gate_weight.shape[0]
    group_count = lax.axis_size("expert")
    expert_total = local_count * group_count
    slot_cap = tok_count * route_top // expert_total
    slot_total = expert_total * slot_cap
    route_count = tok_count * route_top
    target = jnp.where(kept_mask > 0, expert_ids * slot_cap + slot_ids, slot_total).reshape(-1)
    table = (
        jnp.full((slot_total,), route_count, jnp.int32)
        .at[target]
        .set(jnp.arange(route_count, dtype=jnp.int32), mode="drop")
    )
    owner = table // route_top
    tokens_pad = jnp.concatenate([tokens, jnp.zeros((1, model_width), tokens.dtype)], 0)
    cotangent_pad = jnp.concatenate([cotangent, jnp.zeros((1, model_width), cotangent.dtype)], 0)
    weight_pad = jnp.concatenate([route_weights.reshape(-1), jnp.zeros((1,), jnp.float32)], 0)
    x_send = tokens_pad[owner].reshape(group_count, local_count * slot_cap, model_width)
    dy_send = (cotangent_pad[owner].astype(jnp.float32) * weight_pad[table][:, None]).astype(
        jnp.bfloat16
    )
    dy_send = dy_send.reshape(group_count, local_count * slot_cap, model_width)
    full_basis = lax.all_gather(
        projector_basis.astype(jnp.bfloat16), "expert", axis=0, tiled=True
    ).astype(projector_basis.dtype)
    projector = (full_basis * (1.0 / math.sqrt(model_width))).astype(jnp.bfloat16)
    block_shape = (group_count, local_count, slot_cap, model_width)
    x_recv, dy_recv = (
        lax.all_to_all(x_send, "expert", split_axis=0, concat_axis=0, tiled=True),
        lax.all_to_all(dy_send, "expert", split_axis=0, concat_axis=0, tiled=True),
    )
    x_rows = x_recv.reshape(block_shape)
    gate = jnp.einsum("sjcd,jdf->sjcf", x_rows, gate_weight, preferred_element_type=jnp.float32)
    upper = jnp.einsum("sjcd,jdf->sjcf", x_rows, up_weight, preferred_element_type=jnp.float32)
    sigma = jax.nn.sigmoid(gate)
    activated = gate * sigma
    slope = sigma * (1.0 + gate * (1.0 - sigma))
    hidden = (activated * upper).astype(jnp.bfloat16)
    x_proj = jnp.einsum(
        "sjcd,dr->sjcr", x_rows, projector, preferred_element_type=jnp.float32
    ).astype(jnp.bfloat16)
    x_rows, upper, activated, slope, hidden, x_proj = (
        x_rows,
        upper,
        activated,
        slope,
        hidden,
        x_proj,
    )
    dy_rows = dy_recv.reshape(block_shape)
    hidden_grad = jnp.einsum(
        "sjcd,jfd->sjcf", dy_rows, down_weight, preferred_element_type=jnp.float32
    )
    up_grad = (hidden_grad * activated).astype(jnp.bfloat16)
    gate_grad = (hidden_grad * upper * slope).astype(jnp.bfloat16)
    row_grads = jnp.einsum(
        "sjcf,jdf->sjcd", gate_grad, gate_weight, preferred_element_type=jnp.float32
    )
    row_grads = row_grads + jnp.einsum(
        "sjcf,jdf->sjcd", up_grad, up_weight, preferred_element_type=jnp.float32
    )
    row_grads = row_grads.astype(jnp.bfloat16).reshape(
        group_count, local_count * slot_cap, model_width
    )
    returned = lax.all_to_all(row_grads, "expert", split_axis=0, concat_axis=0, tiled=True).reshape(
        slot_total, model_width
    )
    returned = jnp.concatenate([returned, jnp.zeros((1, model_width), jnp.bfloat16)], 0)
    token_grads = jnp.sum(
        returned[target].reshape(tok_count, route_top, model_width).astype(jnp.float32), axis=1
    ).astype(jnp.bfloat16)
    dy_proj = jnp.einsum(
        "sjcd,dr->sjcr", dy_rows, projector, preferred_element_type=jnp.float32
    ).astype(jnp.bfloat16)
    partial_grads = jnp.stack(
        [
            jnp.einsum("sjcf,sjcr->jfr", gate_grad, x_proj, preferred_element_type=jnp.float32),
            jnp.einsum("sjcf,sjcr->jfr", up_grad, x_proj, preferred_element_type=jnp.float32),
            jnp.einsum("sjcf,sjcr->jfr", hidden, dy_proj, preferred_element_type=jnp.float32),
        ],
        1,
    )
    projected_grads = lax.psum(partial_grads, "replica")
    grads_low = projected_grads.astype(jnp.bfloat16)
    mixed = jnp.einsum(
        "sjcf,jfr->sjcr", gate_grad, grads_low[:, 0], preferred_element_type=jnp.float32
    )
    mixed = (
        mixed
        + jnp.einsum("sjcf,jfr->sjcr", up_grad, grads_low[:, 1], preferred_element_type=jnp.float32)
    ).astype(jnp.bfloat16)
    down_mix = jnp.einsum(
        "sjcf,jfr->sjcr", hidden, grads_low[:, 2], preferred_element_type=jnp.float32
    ).astype(jnp.bfloat16)
    power = jnp.einsum("sjcd,sjcr->dr", x_rows, mixed, preferred_element_type=jnp.float32)
    power = power + jnp.einsum(
        "sjcd,sjcr->dr", dy_rows, down_mix, preferred_element_type=jnp.float32
    )
    panel_rows = model_width // group_count
    power_sum = lax.psum(power, ("expert", "replica"))
    gram_total = jnp.dot(
        power_sum.T, power_sum, precision=lax.Precision.HIGHEST, preferred_element_type=jnp.float32
    )
    own_panel = lax.dynamic_slice_in_dim(
        power_sum, lax.axis_index("expert") * panel_rows, panel_rows, 0
    )
    lower = jnp.linalg.cholesky(gram_total)
    new_basis = (
        math.sqrt(model_width) * jax.scipy.linalg.solve_triangular(lower, own_panel.T, lower=True).T
    )
    return (token_grads, projected_grads, new_basis)


def power_of_two(count):
    return count > 1 and count & (count - 1) == 0


def body(*args):
    tok_count, local_count = args[0].shape[0], args[6].shape[0]
    groups, replicas = lax.axis_size("expert"), lax.axis_size("replica")
    slot_cap = tok_count * args[3].shape[1] // (local_count * groups)
    if (
        local_count * slot_cap >= tok_count
        and power_of_two(groups)
        and groups > 2
        and local_count * args[6].shape[2] % 32 == 0
        and replicas == 4
        and args[9].shape[0] % 64 == 0
        and args[9].shape[1] % (32 * groups) == 0
    ):
        return gathered_body(*args)
    return routed_body(*args)


def solution(mesh):
    return jax.shard_map(
        body,
        mesh=mesh,
        in_specs=(
            P(("expert", "replica"), None),
            P(("expert", "replica"), None),
            P(("expert", "replica"), None),
            P(("expert", "replica"), None),
            P(("expert", "replica"), None),
            P(("expert", "replica"), None),
            P("expert", None, None),
            P("expert", None, None),
            P("expert", None, None),
            P("expert", None),
        ),
        out_specs=(
            P(("expert", "replica"), None),
            P("expert", None, None, None),
            P("expert", None),
        ),
        check_vma=False,
    )
```
